256 devices in a mesh: grp: 2 (over y_lo), dp: 8 (over x, core), mp: 16 (over y_hi, z).
Axes of the slice: x: 4, y: 4 (y_hi: 2, y_lo: 2; y = y_hi * 2 + y_lo), z: 8, core: 2. Of those that a mesh axis runs over, the one named last changes fastest.
Arguments:
- teacher_hidden: bfloat16 [32768, 8192], P('dp', 'mp'), may hold values from -6 to 6
- teacher_gain: bfloat16 [8192], P('mp'), may hold values from 0.25 to 1.75
- teacher_value: bfloat16 [8192, 1024], P('mp', 'grp'), may hold values from -0.0625 to 0.0625
- student_hidden: bfloat16 [32768, 4096], P(('dp', 'mp')), may hold values from -24 to 24
- student_gain: bfloat16 [4096], replicated, may hold values from 0.25 to 1.75
- student_value: bfloat16 [4096, 1024], P(('dp', 'mp'), 'grp'), may hold values from -0.09375 to 0.09375
- segment_ids: int32 [32, 1024], P('dp'), may hold values from 0 to 7, never falling along the last dimension, each value on 1 to 384 neighbouring positions
Outputs:
- value_grad: float32 [4096, 1024], P(('dp', 'mp'), 'grp')
The draws below stay inside these ranges and needn't reach their ends.
Inputs may be any that keep to these rules, and one draw needn't show every extreme that they name: `segment_ids`: in every row the ids never fall; each id from 0 to 7 covers 1 to 384 consecutive positions, and one covers exactly 384.
All inputs are finite; a program needn't handle non-finite values.
Results may differ from the reference program's by a relative error of at most 0.0031.
Values may be sent and summed in bfloat16 or wider, within the bound.
A program may use at most 64 MiB of HBM per device.

```python
import math
import jax
import jax.numpy as jnp
import numpy as np
from jax import lax

DT = 8192
DS = 4096
KV = 1024
LEN = 1024
NSEG = 8
MOST = 384
TOKENS = 32768
ROWS = 32


def raised(array, own_key, source, target, blocks, factor):
    def block_of(dim):
        return (jnp.arange(array.shape[dim]) // (array.shape[dim] // blocks)).reshape((-1,) + (1,) * (array.ndim - 1 - dim))

    near = jax.random.permutation(own_key, blocks)[block_of(target)]
    other_side = (block_of(target) + blocks // 2) % blocks
    return jnp.where((block_of(source) == near) | (block_of(source) == other_side), factor * array, array)


def block_scale(stream_key, dims, cuts, least, largest):
    gain, own = 1.0, jax.random.fold_in(stream_key, 6)
    for dim, blocks in cuts:
        steps = jnp.exp(jax.random.uniform(jax.random.fold_in(own, dim), (blocks,), jnp.float32, least / len(cuts), largest / len(cuts)))
        gain = gain * jnp.repeat(steps, dims[dim] // blocks).reshape([-1 if axis == dim else 1 for axis in range(len(dims))])
    return gain


def length_profile(count, total, limit, slope):
    loads = [(1 << 20) // math.isqrt(grade ** slope) + 1 for grade in range(2, count + 1)]
    surplus, given = total - limit - (count - 1), [1] * (count - 1)
    while surplus > 0:
        movable = [i for i in range(count - 1) if given[i] < limit]
        whole, budget = sum([loads[i] for i in movable]), surplus
        for i in movable:
            addition = min(limit - given[i], max(1, budget * loads[i] // whole), surplus)
            given[i] = given[i] + addition
            surplus = surplus - addition
    return np.array([limit] + given)


def ragged_sizes(stream_key, number_of, total, reach, skew):
    if number_of == 2:
        one = jax.random.randint(stream_key, (), max(1, total - reach), min(reach, total - 1) + 1)
        return jnp.stack([one, total - one])
    lengths = jnp.asarray(length_profile(number_of, total, reach, skew), jnp.int32)
    twos = (number_of - 1) // 2
    source_of, sink = lengths[1:1 + 2 * twos:2], lengths[2:2 + 2 * twos:2]
    margin = jnp.minimum(source_of - 1, reach - sink)
    passed = jax.random.randint(jax.random.fold_in(stream_key, 1), (twos,), 0, 1 << 20) % (margin + 1)
    lengths = lengths.at[1:1 + 2 * twos:2].set(source_of - passed).at[2:2 + 2 * twos:2].set(sink + passed)
    return lengths[jax.random.permutation(jax.random.fold_in(stream_key, 2), number_of)]


def bell_draw(rng, extent, width, limit, shards=(), held_as=jnp.bfloat16):
    result = width * jax.random.normal(rng, extent, jnp.float32)
    if shards:
        result = result * block_scale(rng, extent, shards, -0.22, 0.18)
    return jnp.clip(result, -limit, limit).astype(held_as)


def gaussian_with(stream_key, extent, scale, bound, shards, heavy, kind=jnp.bfloat16):
    drawn = scale * jax.random.normal(stream_key, extent, jnp.float32)
    if shards:
        drawn = drawn * block_scale(stream_key, extent, shards, -0.22, 0.18)
    return jnp.clip(raised(drawn, jax.random.fold_in(stream_key, 3), *heavy), -bound, bound).astype(kind)


def setup_inputs(seed: int = 0) -> dict:
    key_list = jax.random.split(jax.random.key(seed), 8)
    return {
        "teacher_hidden": bell_draw(key_list[0], (TOKENS, DT), 1.0, 6.0, ((0, 8), (1, 16))),
        "teacher_gain": jnp.clip(1.0 + 0.15 * jax.random.normal(key_list[1], (DT,), jnp.float32), 0.25, 1.75).astype(jnp.bfloat16),
        "teacher_value": bell_draw(key_list[2], (DT, KV), DT ** -0.5, 0.0625, ((0, 16), (1, 2))),
        "student_hidden": gaussian_with(key_list[3], (TOKENS, DS), 1.0, 24.0, ((0, 128),), (0, 1, 128, 5.5)),
        "student_gain": jnp.clip(1.0 + 0.15 * jax.random.normal(key_list[4], (DS,), jnp.float32), 0.25, 1.75).astype(jnp.bfloat16),
        "student_value": bell_draw(key_list[5], (DS, KV), DS ** -0.5, 0.09375, ((0, 128), (1, 2))),
        "segment_ids": jax.vmap(lambda own: jnp.searchsorted(jnp.cumsum(ragged_sizes(own, NSEG, LEN, MOST, 2)), jnp.arange(LEN), side="right"))(jax.random.split(key_list[6], ROWS)).reshape((ROWS, LEN)).astype(jnp.int32),
    }


norm_eps = 1e-05
power_eps = 1e-06

def row_gradient(teacher_row, student_row, segment_row, teacher_gain, teacher_value, student_gain, student_value):
    teacher_wide = teacher_row.astype(jnp.float32)
    scaled = (teacher_wide * teacher_gain.astype(jnp.float32)).astype(jnp.bfloat16)
    teacher_scale = lax.rsqrt(lax.optimization_barrier(jnp.mean(teacher_wide * teacher_wide, axis=1, keepdims=True)) + norm_eps)
    target = jnp.dot(scaled, teacher_value, preferred_element_type=jnp.float32) * teacher_scale
    target_power = lax.optimization_barrier(jnp.mean(target * target, axis=1, keepdims=True)) + power_eps
    student_wide = student_row.astype(jnp.float32)
    student_scale = lax.rsqrt(lax.optimization_barrier(jnp.mean(student_wide * student_wide, axis=1, keepdims=True)) + norm_eps)
    normed = (student_wide * student_scale * student_gain.astype(jnp.float32)).astype(jnp.bfloat16)
    states = jnp.dot(normed, student_value, preferred_element_type=jnp.float32)
    matches = segment_row[:, None] == jnp.arange(NSEG, dtype=jnp.int32)[None, :]
    counts = lax.optimization_barrier(jnp.sum(matches.astype(jnp.int32), axis=0))
    doc_length = lax.optimization_barrier(jnp.sum(jnp.where(matches, counts[None, :], 0), axis=1)).astype(jnp.float32)
    weighted = ((states - target) / (doc_length[:, None] * target_power)).astype(jnp.bfloat16)
    return jnp.dot(normed.T, weighted, preferred_element_type=jnp.float32)

def reference(teacher_hidden, teacher_gain, teacher_value, student_hidden, student_gain, student_value, segment_ids):
    teacher_rows = teacher_hidden.reshape(ROWS, LEN, DT)
    student_rows = student_hidden.reshape(ROWS, LEN, DS)

    def advance(running, items):
        teacher_row, student_row, segment_row = items
        update = row_gradient(teacher_row, student_row, segment_row, teacher_gain, teacher_value, student_gain, student_value)
        return (running + update, None)
    running, unused = lax.scan(advance, jnp.zeros((DS, KV), jnp.float32), (teacher_rows, student_rows, segment_ids))
    return running
```

```python
import jax
import jax.numpy as jnp
from jax import lax
from jax.experimental import pallas as pl
from jax.experimental.pallas import tpu as pltpu
from jax.sharding import PartitionSpec as P

DT = 8192
DS = 4096
KV = 1024
NSEG = 8
MESH = pl.DeviceIdType.MESH
F32 = jnp.float32
BF16 = jnp.bfloat16

norm_eps = 1e-05
power_eps = 1e-06

ORDER = (4, 3, -3, 2, -2, 1, -1, 0)


def kernel(
    hid_ref,
    gain_ref,
    val_ref,
    stu_ref,
    sgain_ref,
    wsh_ref,
    seg_ref,
    out_ref,
    own,
    oth,
    valo,
    gaino,
    nrm,
    nall,
    wgt,
    ring_s,
    ring_r,
    sq_s,
    sq_r,
    states,
    total,
    pow_s,
    pow_r,
    len_row,
    wall,
    grad,
    grad_s,
    grad_r,
    loc_sem,
    hid_ss,
    hid_rs,
    fwd_ss,
    fwd_rs,
    misc_ss,
    misc_rs,
    wz_ss,
    wz_rs,
    wx_ss,
    wx_rs,
    wc_ss,
    wc_rs,
    nrm_ss,
    nrm_rs,
    ring_ss,
    ring_rs,
    sq_ss,
    sq_rs,
    wal_ss,
    wal_rs,
    wac_ss,
    wac_rs,
    grad_ss,
    grad_rs,
):
    g = lax.axis_index("grp")
    dp = lax.axis_index("dp")
    mp = lax.axis_index("mp")
    x, c = dp // 2, dp % 2
    h, z = mp // 8, mp % 8

    def at(grp=None, xx=None, cc=None, hh=None, zz=None):
        return (
            g if grp is None else grp,
            (x if xx is None else xx) * 2 + (c if cc is None else cc),
            (h if hh is None else hh) * 8 + (z if zz is None else zz),
        )

    def rc(src, dst, ss, rs, dev):
        return pltpu.make_async_remote_copy(
            src_ref=src, dst_ref=dst, send_sem=ss, recv_sem=rs, device_id=dev, device_id_type=MESH
        )

    zp = lambda d: lax.rem(z + d + 8, 8)
    xp = lambda e: lax.rem(x + e + 4, 4)
    grp_dev = at(grp=1 - g)
    cross_dev = at(grp=1 - g, hh=1 - h)
    far_dev = at(hh=1 - h)
    core_dev = at(cc=1 - c)

    own_cp = pltpu.make_async_copy(
        hid_ref.at[pl.ds(pl.multiple_of(h * 2048, 2048), 2048), :], own, loc_sem.at[0]
    )
    own_cp.start()
    w_cp = pltpu.make_async_copy(
        wsh_ref, wgt.at[dp, h, pl.ds(pl.multiple_of(z * 32, 32), 32), :], loc_sem.at[1]
    )
    w_cp.start()

    barrier = pltpu.get_barrier_semaphore()
    count = 0
    for d in range(1, 8):
        pl.semaphore_signal(barrier, inc=1, device_id=at(zz=zp(d)), device_id_type=MESH)
        count += 1
    for d in range(8):
        pl.semaphore_signal(barrier, inc=1, device_id=at(hh=1 - h, zz=zp(d)), device_id_type=MESH)
        count += 1
    for e in range(1, 4):
        for cc in range(2):
            pl.semaphore_signal(
                barrier, inc=1, device_id=at(xx=xp(e), cc=cc), device_id_type=MESH
            )
            count += 1
    for dev in (grp_dev, cross_dev, core_dev):
        pl.semaphore_signal(barrier, inc=1, device_id=dev, device_id_type=MESH)
        count += 1
    pl.semaphore_wait(barrier, count)

    half = pl.ds(pl.multiple_of(c * 256, 256), 256)
    half_o = pl.ds(pl.multiple_of((1 - c) * 256, 256), 256)
    val_cp = rc(val_ref.at[half, :], valo.at[half, :], misc_ss.at[0], misc_rs.at[0], far_dev)
    val_cp.start()
    val_fw = rc(valo.at[half, :], valo.at[half, :], misc_ss.at[1], misc_rs.at[1], core_dev)
    val_in = rc(valo.at[half_o, :], valo.at[half_o, :], misc_ss.at[1], misc_rs.at[1], core_dev)
    gain_cp = rc(gain_ref, gaino, misc_ss.at[2], misc_rs.at[2], cross_dev)
    gain_cp.start()
    wrow = lambda hh: wgt.at[dp, hh, pl.ds(pl.multiple_of(z * 32, 32), 32), :]
    w_far = rc(wsh_ref, wrow(h), misc_ss.at[3], misc_rs.at[3], far_dev)
    w_far_in = rc(wsh_ref, wrow(1 - h), misc_ss.at[3], misc_rs.at[3], far_dev)
    w_far.start()

    def hid_rows(hh, i, j):
        return pl.ds(pl.multiple_of(hh * 2048 + zp(ORDER[i]) * 256 + j * 128, 128), 128)

    def loc_rows(i, j):
        return pl.ds(pl.multiple_of(zp(ORDER[i]) * 256 + j * 128, 128), 128)

    hid_out, hid_in, fwd_out, fwd_in = [], [], [], []
    for i in range(8):
        hid_out.append(
            rc(
                hid_ref.at[hid_rows(1 - h, i, 1 - g), :],
                oth.at[loc_rows(i, 1 - g), :],
                hid_ss.at[i],
                hid_rs.at[i],
                cross_dev,
            )
        )
        mine = oth.at[loc_rows(i, g), :]
        theirs = oth.at[loc_rows(i, 1 - g), :]
        hid_in.append(rc(mine, mine, hid_ss.at[i], hid_rs.at[i], cross_dev))
        fwd_out.append(rc(mine, mine, fwd_ss.at[i], fwd_rs.at[i], grp_dev))
        fwd_in.append(rc(theirs, theirs, fwd_ss.at[i], fwd_rs.at[i], grp_dev))
    for i in range(8):
        hid_out[i].start()

    @pl.loop(0, 8)
    def _(i):
        rows = pl.ds(pl.multiple_of(i * 32, 32), 32)
        wide = stu_ref[rows, :].astype(F32)
        scale = lax.rsqrt(jnp.sum(wide * wide, axis=1, keepdims=True) / DS + norm_eps)
        done = (wide * scale * sgain_ref[...]).astype(BF16)
        for b in range(8):
            nrm[b, rows, :] = done[:, b * 512 : (b + 1) * 512]

    def nrm_out(xx, cc):
        to = xx * 2 + cc
        return rc(nrm.at[to], nall.at[dp], nrm_ss.at[to], nrm_rs.at[dp], at(xx=xx, cc=cc))

    def nrm_in(xx, cc):
        fr = xx * 2 + cc
        return rc(nall.at[fr], nall.at[fr], nrm_ss.at[fr], nrm_rs.at[fr], at(xx=xx, cc=cc))

    nrm_own = pltpu.make_async_copy(nrm.at[dp], nall.at[dp], loc_sem.at[2])
    nrm_own.start()
    nrm_out(x, 1 - c).start()
    for e in (1, 3):
        for cc in range(2):
            nrm_out(xp(e), cc).start()

    w_cp.wait()
    w_far_in.wait_recv()

    def wpiece(d):
        return wgt.at[dp, :, pl.ds(pl.multiple_of(zp(d) * 32, 32), 32), :]

    def wz_out(way, s):
        sign = 1 if way == 0 else -1
        piece = wpiece(-sign * s)
        return rc(piece, piece, wz_ss.at[way, s], wz_rs.at[way, s], at(zz=zp(sign)))

    def wz_in(way, s):
        sign = 1 if way == 0 else -1
        piece = wpiece(-sign * (s + 1))
        return rc(piece, piece, wz_ss.at[way, s], wz_rs.at[way, s], at(zz=zp(sign)))

    def wz_step(s):
        if s > 0:
            wz_in(0, s - 1).wait_recv()
            wz_in(1, s - 1).wait_recv()
        wz_out(0, s).start()
        if s < 3:
            wz_out(1, s).start()

    def wblock(xx, cc=None):
        return wgt.at[xx * 2 + (c if cc is None else cc)]

    def wx_out(way):
        return rc(wblock(x), wblock(x), wx_ss.at[way], wx_rs.at[way], at(xx=xp(1 if way == 0 else -1)))

    def wx_in(way):
        b = wblock(xp(-1 if way == 0 else 1))
        return rc(b, b, wx_ss.at[way], wx_rs.at[way], at(xx=xp(1 if way == 0 else -1)))

    def wx_fw(way):
        b = wblock(xp(-1 if way == 0 else 1)).at[way]
        return rc(b, b, wx_ss.at[2 + way], wx_rs.at[2 + way], at(xx=xp(1 if way == 0 else -1)))

    def wx_fin(way):
        b = wblock(xp(2)).at[way]
        return rc(b, b, wx_ss.at[2 + way], wx_rs.at[2 + way], at(xx=xp(1 if way == 0 else -1)))

    def wc_out(e):
        b = wblock(xp(e))
        return rc(b, b, wc_ss.at[e], wc_rs.at[e], core_dev)

    def wc_in(e):
        b = wblock(xp(e), 1 - c)
        return rc(b, b, wc_ss.at[e], wc_rs.at[e], core_dev)

    wz_step(0)

    seg = seg_ref[pl.ds(mp // 4, 1), :]
    lens = jnp.zeros((1, 1024), F32)
    for s in range(NSEG):
        hit = (seg == s).astype(F32)
        lens = lens + hit * jnp.sum(hit, axis=1, keepdims=True)
    len_row[0:1, :] = lens

    eye = lax.broadcasted_iota(jnp.int32, (128, 128), 0) == lax.broadcasted_iota(
        jnp.int32, (128, 128), 1
    )

    def to_row(col):
        return jnp.sum(jnp.where(eye, col, 0.0), axis=0, keepdims=True)

    def to_col(row):
        return jnp.sum(jnp.where(eye, row, 0.0), axis=1, keepdims=True)

    val_cp.wait_recv()
    val_fw.start()
    own_cp.wait()

    def ring_cp(way, s):
        if s == 0:
            cols = pl.ds(way * 256, 256)
            src, dst = ring_s.at[way, s, :, cols], ring_r.at[way, s, :, cols]
        else:
            src, dst = ring_s.at[way, s], ring_r.at[way, s]
        dev = at(zz=zp(1 if way == 0 else -1))
        return rc(src, dst, ring_ss.at[way, s], ring_rs.at[way, s], dev)

    def sq_out(d):
        return rc(sq_s.at[zp(d)], sq_r.at[z], sq_ss.at[zp(d)], sq_rs.at[z], at(zz=zp(d)))

    def sq_in(d):
        return rc(sq_r.at[zp(d)], sq_r.at[zp(d)], sq_ss.at[zp(d)], sq_rs.at[zp(d)], at(zz=zp(d)))

    def chunk(i):
        d = ORDER[i]
        k = zp(d)
        fwd_in[i].wait_recv()
        if d not in (4, 0):
            ring_cp(0 if d > 0 else 1, 3 - abs(d)).wait_recv()
        if d == 0:
            ring_cp(0, 3).wait_recv()
            ring_cp(1, 3).wait_recv()

        @pl.loop(0, 2)
        def _(j):
            rows = pl.ds(pl.multiple_of(k * 256 + j * 128, 128), 128)
            brows = pl.ds(pl.multiple_of(j * 128, 128), 128)
            h1 = own[rows, :].astype(F32)
            h2 = oth[rows, :].astype(F32)
            acc = jnp.dot(
                (h1 * gain_ref[...]).astype(BF16), val_ref[...], preferred_element_type=F32
            )
            acc += jnp.dot((h2 * gaino[...]).astype(BF16), valo[...], preferred_element_type=F32)
            sq = jnp.sum(h1 * h1 + h2 * h2, axis=1, keepdims=True)
            sq_s[k, pl.ds(j, 1), :] = to_row(sq)
            if d == 4:
                ring_s[0, 0, brows, 0:256] = acc[:, 0:256].astype(BF16)
                ring_s[1, 0, brows, 256:512] = acc[:, 256:512].astype(BF16)
            elif d == 0:
                total[brows, :] = (
                    acc + ring_r[0, 3, brows, :].astype(F32) + ring_r[1, 3, brows, :].astype(F32)
                )
            else:
                way, s = (0 if d > 0 else 1), 4 - abs(d)
                if s == 1:
                    cols = slice(way * 256, way * 256 + 256)
                    rest = slice((1 - way) * 256, (1 - way) * 256 + 256)
                    ring_s[way, s, brows, cols] = (
                        acc[:, cols] + ring_r[way, 0, brows, cols].astype(F32)
                    ).astype(BF16)
                    ring_s[way, s, brows, rest] = acc[:, rest].astype(BF16)
                else:
                    ring_s[way, s, brows, :] = (
                        acc + ring_r[way, s - 1, brows, :].astype(F32)
                    ).astype(BF16)

        if d == 4:
            ring_cp(0, 0).start()
            ring_cp(1, 0).start()
        elif d != 0:
            ring_cp(0 if d > 0 else 1, 4 - abs(d)).start()
        if d != 0:
            sq_out(d).start()

    for i in range(9):
        if i < 8:
            hid_in[i].wait_recv()
            fwd_out[i].start()
        if i == 1:
            wz_step(1)
            wz_step(2)
            val_in.wait_recv()
            gain_cp.wait_recv()
        if i == 2:
            wz_step(3)
        if i == 3:
            wz_in(0, 3).wait_recv()
            wx_out(0).start()
            wx_out(1).start()
            wc_out(0).start()
        if i == 7:
            for way in range(2):
                wx_in(way).wait_recv()
                wx_fw(way).start()
            wc_out(1).start()
            wc_out(3).start()
            for cc in range(2):
                nrm_out(xp(2), cc).start()
        if i == 8:
            wx_fin(0).wait_recv()
            wx_fin(1).wait_recv()
            wc_out(2).start()
            for e in range(4):
                wc_in(e).wait_recv()
            states[...] = jnp.zeros_like(states)

            @pl.loop(0, 8)
            def _(b):
                for hh in range(2):
                    states[...] += jnp.dot(
                        nrm[b, :, hh * 256 : hh * 256 + 256],
                        wgt[b, hh],
                        preferred_element_type=F32,
                    )

        if i >= 1:
            chunk(i - 1)

    for d in range(1, 8):
        sq_in(d).wait_recv()
    sq_r[z] = sq_s[z]
    rows_sq = jnp.zeros((8, 128), F32)
    for s in range(8):
        rows_sq = rows_sq + sq_r[s]
    for j in range(2):
        rows = slice(j * 128, (j + 1) * 128)
        scale = lax.rsqrt(to_col(rows_sq[j : j + 1, :]) / DT + norm_eps)
        target = total[rows, :] * scale
        total[rows, :] = target
        pow_s[j : j + 1, :] = to_row(jnp.sum(target * target, axis=1, keepdims=True))
    pow_cp = rc(pow_s, pow_r, misc_ss.at[4], misc_rs.at[4], grp_dev)
    pow_cp.start()
    pow_cp.wait_recv()
    for j in range(2):
        rows = slice(j * 128, (j + 1) * 128)
        power = (pow_s[j : j + 1, :] + pow_r[j : j + 1, :]) / KV + power_eps
        length = len_row[0:1, pl.ds(pl.multiple_of((mp % 4) * 256 + j * 128, 128), 128)]
        div = to_col(length * power)
        wall[dp, rows, :] = ((states[rows, :] - total[rows, :]) / div).astype(BF16)

    def wal_out(e):
        b = wall.at[dp]
        return rc(b, b, wal_ss.at[e - 1], wal_rs.at[e - 1], at(xx=xp(e)))

    def wal_in(e):
        b = wall.at[xp(-e) * 2 + c]
        return rc(b, b, wal_ss.at[e - 1], wal_rs.at[e - 1], at(xx=xp(e)))

    def wac_out(e):
        b = wall.at[xp(-e) * 2 + c]
        return rc(b, b, wac_ss.at[e], wac_rs.at[e], core_dev)

    def wac_in(e):
        b = wall.at[xp(-e) * 2 + 1 - c]
        return rc(b, b, wac_ss.at[e], wac_rs.at[e], core_dev)

    for e in (1, 3, 2):
        wal_out(e).start()
    wac_out(0).start()
    nrm_own.wait()

    def accumulate(slot, first=False):
        part = lax.dot_general(
            nall[slot], wall[slot], (((0,), (0,)), ((), ())), preferred_element_type=F32
        )
        if first:
            grad[...] = part
        else:
            grad[...] += part

    accumulate(dp, True)
    nrm_in(x, 1 - c).wait_recv()
    wac_in(0).wait_recv()
    accumulate(x * 2 + 1 - c)
    for e in (1, 3, 2):
        for cc in range(2):
            nrm_in(xp(-e), cc).wait_recv()
        wal_in(e).wait_recv()
        wac_out(e).start()
        accumulate(xp(-e) * 2 + c)
        wac_in(e).wait_recv()
        accumulate(xp(-e) * 2 + 1 - c)

    for b in range(16):
        grad_s[b] = grad[b * 32 : (b + 1) * 32, :].astype(BF16)

    def grad_out(t):
        to = lax.rem(mp + t, 16)
        return rc(grad_s.at[to], grad_r.at[mp], grad_ss.at[to], grad_rs.at[mp], (g, dp, to))

    def grad_in(t):
        fr = lax.rem(mp + t, 16)
        return rc(grad_r.at[fr], grad_r.at[fr], grad_ss.at[fr], grad_rs.at[fr], (g, dp, fr))

    for t in range(1, 16):
        grad_out(t).start()
    acc = grad[pl.ds(pl.multiple_of(mp * 32, 32), 32), :]
    for t in range(1, 16):
        grad_in(t).wait_recv()
    for t in range(1, 16):
        acc = acc + grad_r[lax.rem(mp + t, 16)].astype(F32)
    out_ref[...] = acc

    val_cp.wait_send()
    val_fw.wait_send()
    gain_cp.wait_send()
    w_far.wait_send()
    pow_cp.wait_send()
    for i in range(8):
        hid_out[i].wait_send()
        fwd_out[i].wait_send()
    for s in range(4):
        wz_out(0, s).wait_send()
        if s < 3:
            wz_out(1, s).wait_send()
        ring_cp(0, s).wait_send()
        ring_cp(1, s).wait_send()
    for way in range(2):
        wx_out(way).wait_send()
        wx_fw(way).wait_send()
    for e in range(4):
        wc_out(e).wait_send()
        wac_out(e).wait_send()
    nrm_out(x, 1 - c).wait_send()
    for e in range(1, 4):
        wal_out(e).wait_send()
        for cc in range(2):
            nrm_out(xp(e), cc).wait_send()
    for d in range(1, 8):
        sq_out(d).wait_send()
    for t in range(1, 16):
        grad_out(t).wait_send()


def per_device(
    teacher_hidden,
    teacher_gain,
    teacher_value,
    student_hidden,
    student_gain,
    student_value,
    segment_ids,
):
    vmem = pl.BlockSpec(memory_space=pltpu.VMEM)
    dma = pltpu.SemaphoreType.DMA
    return pl.pallas_call(
        kernel,
        out_shape=jax.ShapeDtypeStruct((32, 512), F32),
        in_specs=[pl.BlockSpec(memory_space=pl.ANY)] + [vmem] * 6,
        out_specs=vmem,
        scratch_shapes=[
            pltpu.VMEM((2048, 512), BF16),
            pltpu.VMEM((2048, 512), BF16),
            pltpu.VMEM((512, 512), BF16),
            pltpu.VMEM((1, 512), F32),
            pltpu.VMEM((8, 256, 512), BF16),
            pltpu.VMEM((8, 256, 512), BF16),
            pltpu.VMEM((8, 2, 256, 512), BF16),
            pltpu.VMEM((2, 4, 256, 512), BF16),
            pltpu.VMEM((2, 4, 256, 512), BF16),
            pltpu.VMEM((8, 8, 128), F32),
            pltpu.VMEM((8, 8, 128), F32),
            pltpu.VMEM((256, 512), F32),
            pltpu.VMEM((256, 512), F32),
            pltpu.VMEM((8, 128), F32),
            pltpu.VMEM((8, 128), F32),
            pltpu.VMEM((8, 1024), F32),
            pltpu.VMEM((8, 256, 512), BF16),
            pltpu.VMEM((512, 512), F32),
            pltpu.VMEM((16, 32, 512), BF16),
            pltpu.VMEM((16, 32, 512), BF16),
            dma((3,)),
            dma((8,)),
            dma((8,)),
            dma((8,)),
            dma((8,)),
            dma((5,)),
            dma((5,)),
            dma((2, 4)),
            dma((2, 4)),
            dma((4,)),
            dma((4,)),
            dma((4,)),
            dma((4,)),
            dma((8,)),
            dma((8,)),
            dma((2, 4)),
            dma((2, 4)),
            dma((8,)),
            dma((8,)),
            dma((3,)),
            dma((3,)),
            dma((4,)),
            dma((4,)),
            dma((16,)),
            dma((16,)),
        ],
        compiler_params=pltpu.CompilerParams(
            collective_id=0, has_side_effects=True, vmem_limit_bytes=56 * 1024 * 1024
        ),
    )(
        teacher_hidden,
        teacher_gain.astype(F32).reshape(1, -1),
        teacher_value,
        student_hidden,
        student_gain.astype(F32).reshape(1, -1),
        student_value,
        segment_ids,
    )


def solution(mesh):
    return jax.shard_map(
        per_device,
        mesh=mesh,
        in_specs=(
            P("dp", "mp"),
            P("mp"),
            P("mp", "grp"),
            P(("dp", "mp"), None),
            P(),
            P(("dp", "mp"), "grp"),
            P("dp", None),
        ),
        out_specs=P(("dp", "mp"), "grp"),
        check_vma=False,
    )
```

```python
import jax
import jax.numpy as jnp
from jax import lax
from jax.experimental import pallas as pl
from jax.experimental.pallas import tpu as pltpu
from jax.sharding import PartitionSpec as P

DT = 8192
DS = 4096
KV = 1024
NSEG = 8
MESH = pl.DeviceIdType.MESH
F32 = jnp.float32
BF16 = jnp.bfloat16

norm_eps = 1e-05
power_eps = 1e-06

ORDER = (4, 3, -3, 2, -2, 1, -1, 0)
NEAR = (4, 3, -3, 2, -2, 1, -1)


def kernel(
    hid_ref,
    gain_ref,
    val_ref,
    stu_ref,
    sgain_ref,
    wsh_ref,
    seg_ref,
    out_ref,
    own,
    oth,
    valo,
    valt,
    gaino,
    nrm,
    nall,
    wgt,
    ring_s,
    ring_r,
    sq_s,
    sq_r,
    states,
    total,
    pow_s,
    pow_r,
    len_row,
    wall,
    grad,
    grad_s,
    grad_r,
    loc_sem,
    hid_ss,
    hid_rs,
    fwd_ss,
    fwd_rs,
    misc_ss,
    misc_rs,
    val_ss,
    val_rs,
    wz_ss,
    wz_rs,
    wx_ss,
    wx_rs,
    wc_ss,
    wc_rs,
    nrm_ss,
    nrm_rs,
    ring_ss,
    ring_rs,
    sq_ss,
    sq_rs,
    wal_ss,
    wal_rs,
    wac_ss,
    wac_rs,
    grad_ss,
    grad_rs,
):
    g = lax.axis_index("grp")
    dp = lax.axis_index("dp")
    mp = lax.axis_index("mp")
    x, c = dp // 2, dp % 2
    h, z = mp // 8, mp % 8

    def at(grp=None, xx=None, cc=None, hh=None, zz=None):
        return (
            g if grp is None else grp,
            (x if xx is None else xx) * 2 + (c if cc is None else cc),
            (h if hh is None else hh) * 8 + (z if zz is None else zz),
        )

    def rc(src, dst, ss, rs, dev):
        return pltpu.make_async_remote_copy(
            src_ref=src, dst_ref=dst, send_sem=ss, recv_sem=rs, device_id=dev, device_id_type=MESH
        )

    zp = lambda d: lax.rem(z + d + 8, 8)
    xp = lambda e: lax.rem(x + e + 4, 4)
    grp_dev = at(grp=1 - g)
    cross_dev = at(grp=1 - g, hh=1 - h)
    far_dev = at(hh=1 - h)
    core_dev = at(cc=1 - c)

    own_cp = pltpu.make_async_copy(
        hid_ref.at[pl.ds(pl.multiple_of(h * 2048, 2048), 2048), :], own, loc_sem.at[0]
    )
    own_cp.start()
    w_cp = pltpu.make_async_copy(
        wsh_ref, wgt.at[dp, h, pl.ds(pl.multiple_of(z * 32, 32), 32), :], loc_sem.at[1]
    )
    w_cp.start()

    barrier = pltpu.get_barrier_semaphore()
    count = 0
    for d in range(1, 8):
        pl.semaphore_signal(barrier, inc=1, device_id=at(zz=zp(d)), device_id_type=MESH)
        count += 1
    for d in range(8):
        pl.semaphore_signal(barrier, inc=1, device_id=at(hh=1 - h, zz=zp(d)), device_id_type=MESH)
        count += 1
    for e in range(1, 4):
        for cc in range(2):
            pl.semaphore_signal(
                barrier, inc=1, device_id=at(xx=xp(e), cc=cc), device_id_type=MESH
            )
            count += 1
    for dev in (grp_dev, cross_dev, core_dev):
        pl.semaphore_signal(barrier, inc=1, device_id=dev, device_id_type=MESH)
        count += 1

    sgain = sgain_ref[...].astype(F32).reshape(1, DS)

    @pl.loop(0, 8)
    def _(i):
        rows = pl.ds(pl.multiple_of(i * 32, 32), 32)
        wide = stu_ref[rows, :].astype(F32)
        scale = lax.rsqrt(jnp.sum(wide * wide, axis=1, keepdims=True) / DS + norm_eps)
        done = (wide * scale * sgain).astype(BF16)
        for b in range(8):
            nrm[b, rows, :] = done[:, b * 512 : (b + 1) * 512]

    nrm_own = pltpu.make_async_copy(nrm.at[dp], nall.at[dp], loc_sem.at[2])
    nrm_own.start()

    seg = seg_ref[pl.ds(mp // 4, 1), :]
    lens = jnp.zeros((1, 1024), F32)
    for s in range(NSEG):
        hit = (seg == s).astype(F32)
        lens = lens + hit * jnp.sum(hit, axis=1, keepdims=True)
    len_row[0:1, :] = lens

    eye = lax.broadcasted_iota(jnp.int32, (128, 128), 0) == lax.broadcasted_iota(
        jnp.int32, (128, 128), 1
    )

    def to_row(col):
        return jnp.sum(jnp.where(eye, col, 0.0), axis=0, keepdims=True)

    def to_col(row):
        return jnp.sum(jnp.where(eye, row, 0.0), axis=1, keepdims=True)

    pl.semaphore_wait(barrier, count)

    def wz_piece(hh, d):
        return wgt.at[dp, hh, pl.ds(pl.multiple_of(zp(d) * 32, 32), 32), :]

    def wz_out(b, d):
        src = wsh_ref if b == 0 else wz_piece(1 - h, 0)
        dst = wz_piece(h if b == 0 else 1 - h, 0)
        return rc(src, dst, wz_ss.at[b, zp(d)], wz_rs.at[b, z], at(zz=zp(d)))

    def wz_in(b, d):
        piece = wz_piece(h if b == 0 else 1 - h, d)
        return rc(piece, piece, wz_ss.at[b, zp(d)], wz_rs.at[b, zp(d)], at(zz=zp(d)))

    wrow = lambda hh: wz_piece(hh, 0)
    w_far = rc(wsh_ref, wrow(h), misc_ss.at[3], misc_rs.at[3], far_dev)
    w_far_in = rc(wsh_ref, wrow(1 - h), misc_ss.at[3], misc_rs.at[3], far_dev)
    w_far.start()
    hop1_dev = at(grp=1 - g, hh=(1 - h) * (1 - c) + h * c)
    hop2_dev = at(grp=1 - g, hh=h * (1 - c) + (1 - h) * c)

    def vrows(cc, p):
        return pl.ds(pl.multiple_of(cc * 256 + p * 128, 128), 128)

    val_cp, val_h2, val_fw, val_in = [], [], [], []
    for p in range(2):
        tmp = valt.at[pl.ds(p * 128, 128), :]
        mine, theirs = valo.at[vrows(c, p), :], valo.at[vrows(1 - c, p), :]
        val_cp.append(rc(val_ref.at[vrows(c, p), :], tmp, val_ss.at[0, p], val_rs.at[0, p], hop1_dev))
        val_h2.append(rc(tmp, mine, val_ss.at[1, p], val_rs.at[1, p], hop2_dev))
        val_fw.append(rc(mine, mine, val_ss.at[2, p], val_rs.at[2, p], core_dev))
        val_in.append(rc(theirs, theirs, val_ss.at[2, p], val_rs.at[2, p], core_dev))
        val_cp[p].start()
    gain_cp = rc(gain_ref, gaino, misc_ss.at[2], misc_rs.at[2], cross_dev)
    gain_cp.start()

    def hid_rows(hh, i, j):
        return pl.ds(pl.multiple_of(hh * 2048 + zp(ORDER[i]) * 256 + j * 128, 128), 128)

    def loc_rows(i, j):
        return pl.ds(pl.multiple_of(zp(ORDER[i]) * 256 + j * 128, 128), 128)

    hid_out, hid_in, fwd_out, fwd_in = [], [], [], []
    for i in range(8):
        hid_out.append(
            rc(
                hid_ref.at[hid_rows(1 - h, i, 1 - g), :],
                oth.at[loc_rows(i, 1 - g), :],
                hid_ss.at[i],
                hid_rs.at[i],
                cross_dev,
            )
        )
        mine = oth.at[loc_rows(i, g), :]
        theirs = oth.at[loc_rows(i, 1 - g), :]
        hid_in.append(rc(mine, mine, hid_ss.at[i], hid_rs.at[i], cross_dev))
        fwd_out.append(rc(mine, mine, fwd_ss.at[i], fwd_rs.at[i], grp_dev))
        fwd_in.append(rc(theirs, theirs, fwd_ss.at[i], fwd_rs.at[i], grp_dev))
    for d in NEAR:
        wz_out(0, d).start()
    hid_out[0].start()

    def nrm_out(xx, cc):
        to = xx * 2 + cc
        return rc(nrm.at[to], nall.at[dp], nrm_ss.at[to], nrm_rs.at[dp], at(xx=xx, cc=cc))

    def nrm_in(xx, cc):
        fr = xx * 2 + cc
        return rc(nall.at[fr], nall.at[fr], nrm_ss.at[fr], nrm_rs.at[fr], at(xx=xx, cc=cc))

    nrm_out(x, 1 - c).start()
    for e in (1, 3):
        for cc in range(2):
            nrm_out(xp(e), cc).start()
    nrm_out(xp(2), c).start()

    def wblock(xx, cc=None):
        return wgt.at[xx * 2 + (c if cc is None else cc)]

    def wx_dev(way):
        return at(xx=xp(1 if way == 0 else -1))

    def wx_out(way):
        return rc(wblock(x), wblock(x), wx_ss.at[way], wx_rs.at[way], wx_dev(way))

    def wx_in(way):
        b = wblock(xp(-1 if way == 0 else 1))
        return rc(b, b, wx_ss.at[way], wx_rs.at[way], wx_dev(way))

    def wx_fw(way):
        b = wblock(xp(-1 if way == 0 else 1)).at[way]
        return rc(b, b, wx_ss.at[2 + way], wx_rs.at[2 + way], wx_dev(way))

    def wx_fin(way):
        b = wblock(xp(2)).at[way]
        return rc(b, b, wx_ss.at[2 + way], wx_rs.at[2 + way], wx_dev(way))

    def wc_out(e):
        b = wblock(xp(e))
        return rc(b, b, wc_ss.at[e], wc_rs.at[e], core_dev)

    def wc_in(e):
        b = wblock(xp(e), 1 - c)
        return rc(b, b, wc_ss.at[e], wc_rs.at[e], core_dev)

    def ring_cp(way, s, u):
        rows = pl.ds(pl.multiple_of((g if u == 0 else 1 - g) * 128, 128), 128)
        cols = pl.ds(way * 256, 256) if s == 0 else pl.ds(0, 512)
        dev = at(zz=zp(1 if way == 0 else -1))
        return rc(
            ring_s.at[way, s, rows, cols],
            ring_r.at[way, s, rows, cols],
            ring_ss.at[way, s, u],
            ring_rs.at[way, s, u],
            dev,
        )

    def sq_out(d):
        return rc(sq_s.at[zp(d)], sq_r.at[z], sq_ss.at[zp(d)], sq_rs.at[z], at(zz=zp(d)))

    def sq_in(d):
        return rc(sq_r.at[zp(d)], sq_r.at[zp(d)], sq_ss.at[zp(d)], sq_rs.at[zp(d)], at(zz=zp(d)))

    def sub(i, u):
        d = ORDER[i]
        k = zp(d)
        j = g if u == 0 else 1 - g
        if u == 1:
            fwd_in[i].wait_recv()
        if d == 0:
            ring_cp(0, 3, u).wait_recv()
            ring_cp(1, 3, u).wait_recv()
        elif d != 4:
            ring_cp(0 if d > 0 else 1, 3 - abs(d), u).wait_recv()
        rows = pl.ds(pl.multiple_of(k * 256 + j * 128, 128), 128)
        brows = pl.ds(pl.multiple_of(j * 128, 128), 128)
        h1 = own[rows, :].astype(F32)
        h2 = oth[rows, :].astype(F32)
        tgain = gain_ref[...].astype(F32).reshape(1, 512)
        tgaino = gaino[...].astype(F32).reshape(1, 512)
        acc = jnp.dot((h1 * tgain).astype(BF16), val_ref[...], preferred_element_type=F32)
        acc += jnp.dot((h2 * tgaino).astype(BF16), valo[...], preferred_element_type=F32)
        if d == 4:
            ring_s[0, 0, brows, 0:256] = acc[:, 0:256].astype(BF16)
            ring_s[1, 0, brows, 256:512] = acc[:, 256:512].astype(BF16)
            ring_cp(0, 0, u).start()
            ring_cp(1, 0, u).start()
        elif d == 0:
            total[brows, :] = (
                acc + ring_r[0, 3, brows, :].astype(F32) + ring_r[1, 3, brows, :].astype(F32)
            )
        else:
            way, s = (0 if d > 0 else 1), 4 - abs(d)
            if s == 1:
                cols = slice(way * 256, way * 256 + 256)
                rest = slice((1 - way) * 256, (1 - way) * 256 + 256)
                ring_s[way, s, brows, cols] = (
                    acc[:, cols] + ring_r[way, 0, brows, cols].astype(F32)
                ).astype(BF16)
                ring_s[way, s, brows, rest] = acc[:, rest].astype(BF16)
            else:
                ring_s[way, s, brows, :] = (
                    acc + ring_r[way, s - 1, brows, :].astype(F32)
                ).astype(BF16)
            ring_cp(way, s, u).start()
        sq = jnp.sum(h1 * h1 + h2 * h2, axis=1, keepdims=True)
        sq_s[k, pl.ds(j, 1), :] = to_row(sq)
        if u == 1 and d != 0:
            sq_out(d).start()

    def take(i):
        hid_in[i].wait_recv()
        fwd_out[i].start()
        if i + 3 < 8:
            hid_out[i + 3].start()

    def add_states(blocks):
        part = None
        for b in blocks:
            for hh in range(2):
                t = jnp.dot(
                    nrm[b, :, hh * 256 : hh * 256 + 256], wgt[b, hh], preferred_element_type=F32
                )
                part = t if part is None else part + t
        states[...] += part

    states[...] = jnp.zeros_like(states)
    w_far_in.wait_recv()
    for d in NEAR:
        wz_out(1, d).start()
    for p in range(2):
        val_cp[p].wait_recv()
        val_h2[p].start()
    hid_out[1].start()
    hid_out[2].start()
    take(0)
    for p in range(2):
        val_h2[p].wait_recv()
        val_fw[p].start()
    own_cp.wait()
    w_cp.wait()
    gain_cp.wait_recv()
    for p in range(2):
        val_in[p].wait_recv()
    sub(0, 0)
    for b in range(2):
        for d in NEAR:
            wz_in(b, d).wait_recv()
    wx_out(0).start()
    wx_out(1).start()
    wc_out(0).start()
    take(1)
    take(2)
    sub(0, 1)
    sub(1, 0)
    sub(2, 0)
    take(3)
    sub(1, 1)
    sub(2, 1)
    take(4)
    sub(3, 0)
    sub(4, 0)
    for way in range(2):
        wx_in(way).wait_recv()
        wx_fw(way).start()
    wc_out(1).start()
    wc_out(3).start()
    take(5)
    sub(3, 1)
    sub(4, 1)
    take(6)
    add_states((xp(1) * 2 + c, xp(-1) * 2 + c))
    wc_in(0).wait_recv()
    add_states((dp, x * 2 + 1 - c))
    sub(5, 0)
    sub(6, 0)
    take(7)
    sub(5, 1)
    sub(6, 1)
    wx_fin(0).wait_recv()
    wx_fin(1).wait_recv()
    wc_out(2).start()
    nrm_out(xp(2), 1 - c).start()
    wc_in(1).wait_recv()
    wc_in(3).wait_recv()
    add_states((xp(1) * 2 + 1 - c, xp(-1) * 2 + 1 - c))
    sub(7, 0)
    sub(7, 1)
    wc_in(2).wait_recv()
    add_states((xp(2) * 2, xp(2) * 2 + 1))

    for d in range(1, 8):
        sq_in(d).wait_recv()
    sq_r[z] = sq_s[z]
    rows_sq = jnp.zeros((8, 128), F32)
    for s in range(8):
        rows_sq = rows_sq + sq_r[s]
    for j in range(2):
        rows = slice(j * 128, (j + 1) * 128)
        scale = lax.rsqrt(to_col(rows_sq[j : j + 1, :]) / DT + norm_eps)
        target = total[rows, :] * scale
        total[rows, :] = states[rows, :] - target
        pow_s[j : j + 1, :] = to_row(jnp.sum(target * target, axis=1, keepdims=True))
    pow_cp = rc(pow_s, pow_r, misc_ss.at[4], misc_rs.at[4], grp_dev)
    pow_cp.start()

    def wal_out(q, e):
        b = wall.at[q, dp]
        return rc(b, b, wal_ss.at[q, e - 1], wal_rs.at[q, e - 1], at(xx=xp(e)))

    def wal_in(q, e):
        b = wall.at[q, xp(-e) * 2 + c]
        return rc(b, b, wal_ss.at[q, e - 1], wal_rs.at[q, e - 1], at(xx=xp(e)))

    def wac_out(q, e):
        b = wall.at[q, xp(-e) * 2 + c]
        return rc(b, b, wac_ss.at[q, e], wac_rs.at[q, e], core_dev)

    def wac_in(q, e):
        b = wall.at[q, xp(-e) * 2 + 1 - c]
        return rc(b, b, wac_ss.at[q, e], wac_rs.at[q, e], core_dev)

    def grad_out(q, t):
        to = lax.rem(mp + t, 16)
        return rc(
            grad_s.at[q, to], grad_r.at[q, mp], grad_ss.at[q, to], grad_rs.at[q, mp], (g, dp, to)
        )

    def grad_in(q, t):
        fr = lax.rem(mp + t, 16)
        return rc(
            grad_r.at[q, fr], grad_r.at[q, fr], grad_ss.at[q, fr], grad_rs.at[q, fr], (g, dp, fr)
        )

    pow_cp.wait_recv()
    divs = []
    for j in range(2):
        power = (pow_s[j : j + 1, :] + pow_r[j : j + 1, :]) / KV + power_eps
        length = len_row[0:1, pl.ds(pl.multiple_of((mp % 4) * 256 + j * 128, 128), 128)]
        divs.append(to_col(length * power))
    for q in range(2):
        for j in range(2):
            rows = slice(j * 128, (j + 1) * 128)
            wall[q, dp, rows, :] = (total[rows, q * 256 : q * 256 + 256] / divs[j]).astype(BF16)
        for e in (1, 3, 2):
            wal_out(q, e).start()
        wac_out(q, 0).start()

    nrm_own.wait()
    nrm_in(x, 1 - c).wait_recv()
    for e in (1, 3, 2):
        for cc in range(2):
            nrm_in(xp(-e), cc).wait_recv()

    def accumulate(q, slot):
        grad[...] += lax.dot_general(
            nall[slot], wall[q, slot], (((0,), (0,)), ((), ())), preferred_element_type=F32
        )

    for q in range(2):
        grad[...] = jnp.zeros_like(grad)
        accumulate(q, dp)
        wac_in(q, 0).wait_recv()
        accumulate(q, x * 2 + 1 - c)
        wal_in(q, 1).wait_recv()
        wac_out(q, 1).start()
        accumulate(q, xp(-1) * 2 + c)
        wal_in(q, 3).wait_recv()
        wac_out(q, 3).start()
        accumulate(q, xp(-3) * 2 + c)
        wac_in(q, 1).wait_recv()
        accumulate(q, xp(-1) * 2 + 1 - c)
        wal_in(q, 2).wait_recv()
        wac_out(q, 2).start()
        accumulate(q, xp(-2) * 2 + c)
        wac_in(q, 3).wait_recv()
        accumulate(q, xp(-3) * 2 + 1 - c)
        wac_in(q, 2).wait_recv()
        accumulate(q, xp(-2) * 2 + 1 - c)
        for b in range(16):
            grad_s[q, b] = grad[b * 32 : (b + 1) * 32, :].astype(BF16)
        for t in range(1, 16):
            grad_out(q, t).start()
        out_ref[:, q * 256 : q * 256 + 256] = grad[pl.ds(pl.multiple_of(mp * 32, 32), 32), :]

    for q in range(2):
        for t in range(1, 16):
            grad_in(q, t).wait_recv()
        acc = out_ref[:, q * 256 : q * 256 + 256]
        for t in range(1, 16):
            acc = acc + grad_r[q, lax.rem(mp + t, 16)].astype(F32)
        out_ref[:, q * 256 : q * 256 + 256] = acc

    for p in range(2):
        val_cp[p].wait_send()
        val_h2[p].wait_send()
        val_fw[p].wait_send()
    gain_cp.wait_send()
    w_far.wait_send()
    pow_cp.wait_send()
    for i in range(8):
        hid_out[i].wait_send()
        fwd_out[i].wait_send()
    for d in NEAR:
        wz_out(0, d).wait_send()
        wz_out(1, d).wait_send()
    for s in range(4):
        for u in range(2):
            ring_cp(0, s, u).wait_send()
            ring_cp(1, s, u).wait_send()
    for way in range(2):
        wx_out(way).wait_send()
        wx_fw(way).wait_send()
    for e in range(4):
        wc_out(e).wait_send()
        for q in range(2):
            wac_out(q, e).wait_send()
    nrm_out(x, 1 - c).wait_send()
    for e in range(1, 4):
        for q in range(2):
            wal_out(q, e).wait_send()
        for cc in range(2):
            nrm_out(xp(e), cc).wait_send()
    for d in range(1, 8):
        sq_out(d).wait_send()
    for q in range(2):
        for t in range(1, 16):
            grad_out(q, t).wait_send()


def per_device(
    teacher_hidden,
    teacher_gain,
    teacher_value,
    student_hidden,
    student_gain,
    student_value,
    segment_ids,
):
    vmem = pl.BlockSpec(memory_space=pltpu.VMEM)
    dma = pltpu.SemaphoreType.DMA
    return pl.pallas_call(
        kernel,
        out_shape=jax.ShapeDtypeStruct((32, 512), F32),
        in_specs=[pl.BlockSpec(memory_space=pl.ANY)] + [vmem] * 6,
        out_specs=vmem,
        scratch_shapes=[
            pltpu.VMEM((2048, 512), BF16),
            pltpu.VMEM((2048, 512), BF16),
            pltpu.VMEM((512, 512), BF16),
            pltpu.VMEM((256, 512), BF16),
            pltpu.VMEM((512,), BF16),
            pltpu.VMEM((8, 256, 512), BF16),
            pltpu.VMEM((8, 256, 512), BF16),
            pltpu.VMEM((8, 2, 256, 512), BF16),
            pltpu.VMEM((2, 4, 256, 512), BF16),
            pltpu.VMEM((2, 4, 256, 512), BF16),
            pltpu.VMEM((8, 8, 128), F32),
            pltpu.VMEM((8, 8, 128), F32),
            pltpu.VMEM((256, 512), F32),
            pltpu.VMEM((256, 512), F32),
            pltpu.VMEM((8, 128), F32),
            pltpu.VMEM((8, 128), F32),
            pltpu.VMEM((8, 1024), F32),
            pltpu.VMEM((2, 8, 256, 256), BF16),
            pltpu.VMEM((512, 256), F32),
            pltpu.VMEM((2, 16, 32, 256), BF16),
            pltpu.VMEM((2, 16, 32, 256), BF16),
            dma((3,)),
            dma((8,)),
            dma((8,)),
            dma((8,)),
            dma((8,)),
            dma((5,)),
            dma((5,)),
            dma((3, 2)),
            dma((3, 2)),
            dma((2, 8)),
            dma((2, 8)),
            dma((4,)),
            dma((4,)),
            dma((4,)),
            dma((4,)),
            dma((8,)),
            dma((8,)),
            dma((2, 4, 2)),
            dma((2, 4, 2)),
            dma((8,)),
            dma((8,)),
            dma((2, 3)),
            dma((2, 3)),
            dma((2, 4)),
            dma((2, 4)),
            dma((2, 16)),
            dma((2, 16)),
        ],
        compiler_params=pltpu.CompilerParams(
            collective_id=0, has_side_effects=True, vmem_limit_bytes=56 * 1024 * 1024
        ),
    )(
        teacher_hidden,
        teacher_gain,
        teacher_value,
        student_hidden,
        student_gain,
        student_value,
        segment_ids,
    )


def solution(mesh):
    return jax.shard_map(
        per_device,
        mesh=mesh,
        in_specs=(
            P("dp", "mp"),
            P("mp"),
            P("mp", "grp"),
            P(("dp", "mp"), None),
            P(),
            P(("dp", "mp"), "grp"),
            P("dp", None),
        ),
        out_specs=P(("dp", "mp"), "grp"),
        check_vma=False,
    )
```

```python
import jax
import jax.numpy as jnp
from jax import lax
from jax.experimental import pallas as pl
from jax.experimental.pallas import tpu as pltpu
from jax.sharding import PartitionSpec as P

DT = 8192
DS = 4096
KV = 1024
NSEG = 8
MESH = pl.DeviceIdType.MESH
F32 = jnp.float32
BF16 = jnp.bfloat16

norm_eps = 1e-05
power_eps = 1e-06

ORDER = (4, 3, -3, 2, -2, 1, -1, 0)
NQ = 4
QW = 512 // NQ
NEAR = (4, 3, -3, 2, -2, 1, -1)


def kernel(
    hid_ref,
    gain_ref,
    val_ref,
    stu_ref,
    sgain_ref,
    wsh_ref,
    seg_ref,
    out_ref,
    own,
    oth,
    valo,
    gaino,
    nrm,
    nall,
    nturn,
    wgt,
    ring_s,
    ring_r,
    sq_s,
    sq_r,
    states,
    total,
    pow_s,
    pow_r,
    len_row,
    wall,
    grad,
    grad_s,
    grad_r,
    loc_sem,
    hid_ss,
    hid_rs,
    fwd_ss,
    fwd_rs,
    misc_ss,
    misc_rs,
    vx_ss,
    vx_rs,
    vc_ss,
    vc_rs,
    wz_ss,
    wz_rs,
    wx_ss,
    wx_rs,
    wc_ss,
    wc_rs,
    nrm_ss,
    nrm_rs,
    swap_ss,
    swap_rs,
    ring_ss,
    ring_rs,
    sq_ss,
    sq_rs,
    wal_ss,
    wal_rs,
    wac_ss,
    wac_rs,
    grad_ss,
    grad_rs,
):
    g = lax.axis_index("grp")
    dp = lax.axis_index("dp")
    mp = lax.axis_index("mp")
    x, c = dp // 2, dp % 2
    h, z = mp // 8, mp % 8

    def at(grp=None, xx=None, cc=None, hh=None, zz=None):
        return (
            g if grp is None else grp,
            (x if xx is None else xx) * 2 + (c if cc is None else cc),
            (h if hh is None else hh) * 8 + (z if zz is None else zz),
        )

    def rc(src, dst, ss, rs, dev):
        return pltpu.make_async_remote_copy(
            src_ref=src, dst_ref=dst, send_sem=ss, recv_sem=rs, device_id=dev, device_id_type=MESH
        )

    zp = lambda d: lax.rem(z + d + 8, 8)
    xp = lambda e: lax.rem(x + e + 4, 4)
    grp_dev = at(grp=1 - g)
    cross_dev = at(grp=1 - g, hh=1 - h)
    far_dev = at(hh=1 - h)
    core_dev = at(cc=1 - c)

    own_cp = pltpu.make_async_copy(
        hid_ref.at[pl.ds(pl.multiple_of(h * 2048, 2048), 2048), :], own, loc_sem.at[0]
    )
    own_cp.start()
    w_cp = pltpu.make_async_copy(
        wsh_ref, wgt.at[dp, h, pl.ds(pl.multiple_of(z * 32, 32), 32), :], loc_sem.at[1]
    )
    w_cp.start()

    barrier = pltpu.get_barrier_semaphore()
    count = 0
    for d in range(1, 8):
        pl.semaphore_signal(barrier, inc=1, device_id=at(zz=zp(d)), device_id_type=MESH)
        count += 1
    for d in range(8):
        pl.semaphore_signal(barrier, inc=1, device_id=at(hh=1 - h, zz=zp(d)), device_id_type=MESH)
        count += 1
    for e in range(1, 4):
        for cc in range(2):
            pl.semaphore_signal(
                barrier, inc=1, device_id=at(xx=xp(e), cc=cc), device_id_type=MESH
            )
            count += 1
    for dev in (grp_dev, cross_dev, core_dev):
        pl.semaphore_signal(barrier, inc=1, device_id=dev, device_id_type=MESH)
        count += 1

    sgain = sgain_ref[...].astype(F32).reshape(1, DS)

    @pl.loop(0, 8)
    def _(i):
        rows = pl.ds(pl.multiple_of(i * 32, 32), 32)
        wide = stu_ref[rows, :].astype(F32)
        scale = lax.rsqrt(jnp.sum(wide * wide, axis=1, keepdims=True) / DS + norm_eps)
        done = (wide * scale * sgain).astype(BF16)
        for b in range(8):
            nrm[b, rows, :] = done[:, b * 512 : (b + 1) * 512]

    nrm_own = pltpu.make_async_copy(nrm.at[dp], nall.at[dp], loc_sem.at[2])
    nrm_own.start()

    seg = seg_ref[pl.ds(mp // 4, 1), :]
    lens = jnp.zeros((1, 1024), F32)
    for s in range(NSEG):
        hit = (seg == s).astype(F32)
        lens = lens + hit * jnp.sum(hit, axis=1, keepdims=True)
    len_row[0:1, :] = lens

    eye = lax.broadcasted_iota(jnp.int32, (128, 128), 0) == lax.broadcasted_iota(
        jnp.int32, (128, 128), 1
    )

    def to_row(col):
        return jnp.sum(jnp.where(eye, col, 0.0), axis=0, keepdims=True)

    def to_col(row):
        return jnp.sum(jnp.where(eye, row, 0.0), axis=1, keepdims=True)

    pl.semaphore_wait(barrier, count)

    def wz_piece(hh, d):
        return wgt.at[dp, hh, pl.ds(pl.multiple_of(zp(d) * 32, 32), 32), :]

    def wz_out(b, d):
        src = wsh_ref if b == 0 else wz_piece(1 - h, 0)
        dst = wz_piece(h if b == 0 else 1 - h, 0)
        return rc(src, dst, wz_ss.at[b, zp(d)], wz_rs.at[b, z], at(zz=zp(d)))

    def wz_in(b, d):
        piece = wz_piece(h if b == 0 else 1 - h, d)
        return rc(piece, piece, wz_ss.at[b, zp(d)], wz_rs.at[b, zp(d)], at(zz=zp(d)))

    wrow = lambda hh: wz_piece(hh, 0)
    w_far = rc(wsh_ref, wrow(h), misc_ss.at[3], misc_rs.at[3], far_dev)
    w_far_in = rc(wsh_ref, wrow(1 - h), misc_ss.at[3], misc_rs.at[3], far_dev)
    w_far.start()
    def vblock(xx, cc):
        return valo.at[pl.ds(pl.multiple_of((xx * 2 + cc) * 64, 64), 64), :]

    val_cp = rc(
        val_ref.at[pl.ds(pl.multiple_of(dp * 64, 64), 64), :],
        vblock(x, c),
        misc_ss.at[0],
        misc_rs.at[0],
        far_dev,
    )
    val_cp.start()

    def vx_out(e):
        b = vblock(x, c)
        return rc(b, b, vx_ss.at[e], vx_rs.at[e], at(xx=xp(e)))

    def vx_in(e):
        b = vblock(xp(-e), c)
        return rc(b, b, vx_ss.at[e], vx_rs.at[e], at(xx=xp(e)))

    def vc_out(e):
        b = vblock(xp(-e), c)
        return rc(b, b, vc_ss.at[e], vc_rs.at[e], core_dev)

    def vc_in(e):
        b = vblock(xp(-e), 1 - c)
        return rc(b, b, vc_ss.at[e], vc_rs.at[e], core_dev)

    gain_cp = rc(gain_ref, gaino, misc_ss.at[2], misc_rs.at[2], cross_dev)
    gain_cp.start()

    def hid_rows(hh, i, j):
        return pl.ds(pl.multiple_of(hh * 2048 + zp(ORDER[i]) * 256 + j * 128, 128), 128)

    def loc_rows(i, j):
        return pl.ds(pl.multiple_of(zp(ORDER[i]) * 256 + j * 128, 128), 128)

    hid_out, hid_in, fwd_out, fwd_in = [], [], [], []
    for i in range(8):
        hid_out.append(
            rc(
                hid_ref.at[hid_rows(1 - h, i, 1 - g), :],
                oth.at[loc_rows(i, 1 - g), :],
                hid_ss.at[i],
                hid_rs.at[i],
                cross_dev,
            )
        )
        mine = oth.at[loc_rows(i, g), :]
        theirs = oth.at[loc_rows(i, 1 - g), :]
        hid_in.append(rc(mine, mine, hid_ss.at[i], hid_rs.at[i], cross_dev))
        fwd_out.append(rc(mine, mine, fwd_ss.at[i], fwd_rs.at[i], grp_dev))
        fwd_in.append(rc(theirs, theirs, fwd_ss.at[i], fwd_rs.at[i], grp_dev))
    for d in NEAR:
        wz_out(0, d).start()
    for i in range(8):
        hid_out[i].start()

    def nrm_out(xx, cc):
        to = xx * 2 + cc
        return rc(nrm.at[to], nall.at[dp], nrm_ss.at[to], nrm_rs.at[dp], at(xx=xx, cc=cc))

    def nrm_in(xx, cc):
        fr = xx * 2 + cc
        return rc(nall.at[fr], nall.at[fr], nrm_ss.at[fr], nrm_rs.at[fr], at(xx=xx, cc=cc))

    grows = lambda gg: pl.ds(pl.multiple_of(gg * 128, 128), 128)

    def far_out(cc):
        to = xp(2) * 2 + cc
        return rc(
            nrm.at[to, grows(g), :],
            nall.at[dp, grows(g), :],
            nrm_ss.at[to],
            nrm_rs.at[dp],
            at(xx=xp(2), cc=cc),
        )

    def far_in(cc):
        b = nall.at[xp(2) * 2 + cc, grows(g), :]
        return rc(b, b, nrm_ss.at[xp(2) * 2 + cc], nrm_rs.at[xp(2) * 2 + cc], grp_dev)

    def swap_out(cc):
        b = nall.at[xp(2) * 2 + cc, grows(g), :]
        return rc(b, b, swap_ss.at[cc], swap_rs.at[cc], grp_dev)

    def swap_in(cc):
        b = nall.at[xp(2) * 2 + cc, grows(1 - g), :]
        return rc(b, b, swap_ss.at[cc], swap_rs.at[cc], grp_dev)

    nrm_out(x, 1 - c).start()
    for e in (1, 3):
        nrm_out(xp(e), c).start()

    def wblock(xx, cc=None):
        return wgt.at[xx * 2 + (c if cc is None else cc)]

    def wx_dev(way):
        return at(xx=xp(1 if way == 0 else -1))

    def wx_out(way, part):
        b = wblock(x).at[way if part == 0 else 1 - way]
        return rc(b, b, wx_ss.at[part, way], wx_rs.at[part, way], wx_dev(way))

    def wx_in(way, part):
        b = wblock(xp(-1 if way == 0 else 1)).at[way if part == 0 else 1 - way]
        return rc(b, b, wx_ss.at[part, way], wx_rs.at[part, way], wx_dev(way))

    def wx_fw(way):
        b = wblock(xp(-1 if way == 0 else 1)).at[way]
        return rc(b, b, wx_ss.at[2, way], wx_rs.at[2, way], wx_dev(way))

    def wx_fin(way):
        b = wblock(xp(2)).at[way]
        return rc(b, b, wx_ss.at[2, way], wx_rs.at[2, way], wx_dev(way))

    def wc_out(e):
        b = wblock(xp(e))
        return rc(b, b, wc_ss.at[e], wc_rs.at[e], core_dev)

    def wc_in(e):
        b = wblock(xp(e), 1 - c)
        return rc(b, b, wc_ss.at[e], wc_rs.at[e], core_dev)

    def ring_cp(way, s, u):
        rows = pl.ds(pl.multiple_of((g if u == 0 else 1 - g) * 128, 128), 128)
        cols = pl.ds(way * 256, 256) if s == 0 else pl.ds(0, 512)
        dev = at(zz=zp(1 if way == 0 else -1))
        return rc(
            ring_s.at[way, s, rows, cols],
            ring_r.at[way, s, rows, cols],
            ring_ss.at[way, s, u],
            ring_rs.at[way, s, u],
            dev,
        )

    def sq_out(d):
        return rc(sq_s.at[zp(d)], sq_r.at[z], sq_ss.at[zp(d)], sq_rs.at[z], at(zz=zp(d)))

    def sq_in(d):
        return rc(sq_r.at[zp(d)], sq_r.at[zp(d)], sq_ss.at[zp(d)], sq_rs.at[zp(d)], at(zz=zp(d)))

    def sub(i, u):
        d = ORDER[i]
        k = zp(d)
        j = g if u == 0 else 1 - g
        if u == 1:
            fwd_in[i].wait_recv()
        if d == 0:
            ring_cp(0, 3, u).wait_recv()
            ring_cp(1, 3, u).wait_recv()
        elif d != 4:
            ring_cp(0 if d > 0 else 1, 3 - abs(d), u).wait_recv()
        rows = pl.ds(pl.multiple_of(k * 256 + j * 128, 128), 128)
        brows = pl.ds(pl.multiple_of(j * 128, 128), 128)
        h1 = own[rows, :].astype(F32)
        h2 = oth[rows, :].astype(F32)
        tgain = gain_ref[...].astype(F32).reshape(1, 512)
        tgaino = gaino[...].astype(F32).reshape(1, 512)
        acc = jnp.dot((h1 * tgain).astype(BF16), val_ref[...], preferred_element_type=F32)
        acc += jnp.dot((h2 * tgaino).astype(BF16), valo[...], preferred_element_type=F32)
        if d == 4:
            ring_s[0, 0, brows, 0:256] = acc[:, 0:256].astype(BF16)
            ring_s[1, 0, brows, 256:512] = acc[:, 256:512].astype(BF16)
            ring_cp(0, 0, u).start()
            ring_cp(1, 0, u).start()
        elif d == 0:
            total[brows, :] = (
                acc + ring_r[0, 3, brows, :].astype(F32) + ring_r[1, 3, brows, :].astype(F32)
            )
        else:
            way, s = (0 if d > 0 else 1), 4 - abs(d)
            if s == 1:
                cols = slice(way * 256, way * 256 + 256)
                rest = slice((1 - way) * 256, (1 - way) * 256 + 256)
                ring_s[way, s, brows, cols] = (
                    acc[:, cols] + ring_r[way, 0, brows, cols].astype(F32)
                ).astype(BF16)
                ring_s[way, s, brows, rest] = acc[:, rest].astype(BF16)
            else:
                ring_s[way, s, brows, :] = (
                    acc + ring_r[way, s - 1, brows, :].astype(F32)
                ).astype(BF16)
            ring_cp(way, s, u).start()
        sq = jnp.sum(h1 * h1 + h2 * h2, axis=1, keepdims=True)
        sq_s[k, pl.ds(j, 1), :] = to_row(sq)
        if u == 1 and d != 0:
            sq_out(d).start()

    def turn(slot):
        nturn[slot] = nall[slot].T

    def take(i):
        hid_in[i].wait_recv()
        fwd_out[i].start()

    def add_states(blocks):
        part = None
        for b in blocks:
            for hh in range(2):
                t = jnp.dot(
                    nrm[b, :, hh * 256 : hh * 256 + 256], wgt[b, hh], preferred_element_type=F32
                )
                part = t if part is None else part + t
        states[...] += part

    states[...] = jnp.zeros_like(states)
    val_cp.wait_recv()
    for e in (1, 3, 2):
        vx_out(e).start()
    vc_out(0).start()
    for e in (1, 3):
        nrm_out(xp(e), 1 - c).start()
    w_far_in.wait_recv()
    for d in NEAR:
        wz_out(1, d).start()
    take(0)
    for e in (1, 3, 2):
        vx_in(e).wait_recv()
        vc_out(e).start()
    own_cp.wait()
    w_cp.wait()
    gain_cp.wait_recv()
    take(1)
    for e in range(4):
        vc_in(e).wait_recv()
    sub(0, 0)
    sub(0, 1)
    for b in range(2):
        for d in NEAR:
            wz_in(b, d).wait_recv()
    for part in range(2):
        for way in range(2):
            wx_out(way, part).start()
    wc_out(0).start()
    take(2)
    sub(1, 0)
    sub(2, 0)
    take(3)
    nrm_own.wait()
    turn(dp)
    nrm_in(x, 1 - c).wait_recv()
    turn(x * 2 + 1 - c)
    sub(1, 1)
    sub(2, 1)
    take(4)
    sub(3, 0)
    sub(4, 0)
    for way in range(2):
        wx_in(way, 0).wait_recv()
        wx_fw(way).start()
    for cc in range(2):
        far_out(cc).start()
    take(5)
    sub(3, 1)
    sub(4, 1)
    for cc in range(2):
        nrm_in(xp(1), cc).wait_recv()
        turn(xp(1) * 2 + cc)
    take(6)
    wc_in(0).wait_recv()
    add_states((dp, x * 2 + 1 - c))
    sub(5, 0)
    sub(6, 0)
    for way in range(2):
        wx_in(way, 1).wait_recv()
    wc_out(1).start()
    wc_out(3).start()
    add_states((xp(1) * 2 + c, xp(-1) * 2 + c))
    take(7)
    sub(5, 1)
    sub(6, 1)
    for cc in range(2):
        nrm_in(xp(3), cc).wait_recv()
        turn(xp(3) * 2 + cc)
    wc_in(1).wait_recv()
    wc_in(3).wait_recv()
    add_states((xp(1) * 2 + 1 - c, xp(-1) * 2 + 1 - c))
    wx_fin(0).wait_recv()
    wx_fin(1).wait_recv()
    wc_out(2).start()
    sub(7, 0)
    wc_in(2).wait_recv()
    add_states((xp(2) * 2, xp(2) * 2 + 1))
    sub(7, 1)

    for d in range(1, 8):
        sq_in(d).wait_recv()
    sq_r[z] = sq_s[z]
    rows_sq = jnp.zeros((8, 128), F32)
    for s in range(8):
        rows_sq = rows_sq + sq_r[s]
    for j in range(2):
        rows = slice(j * 128, (j + 1) * 128)
        scale = lax.rsqrt(to_col(rows_sq[j : j + 1, :]) / DT + norm_eps)
        target = total[rows, :] * scale
        total[rows, :] = states[rows, :] - target
        pow_s[j : j + 1, :] = to_row(jnp.sum(target * target, axis=1, keepdims=True))
    pow_cp = rc(pow_s, pow_r, misc_ss.at[4], misc_rs.at[4], grp_dev)
    pow_cp.start()

    def wal_out(q, e):
        b = wall.at[q, dp]
        return rc(b, b, wal_ss.at[q, e - 1], wal_rs.at[q, e - 1], at(xx=xp(e)))

    def wal_in(q, e):
        b = wall.at[q, xp(-e) * 2 + c]
        return rc(b, b, wal_ss.at[q, e - 1], wal_rs.at[q, e - 1], at(xx=xp(e)))

    def wac_out(q, e):
        b = wall.at[q, xp(-e) * 2 + c]
        return rc(b, b, wac_ss.at[q, e], wac_rs.at[q, e], core_dev)

    def wac_in(q, e):
        b = wall.at[q, xp(-e) * 2 + 1 - c]
        return rc(b, b, wac_ss.at[q, e], wac_rs.at[q, e], core_dev)

    def grad_out(q, t):
        to = lax.rem(mp + t, 16)
        return rc(
            grad_s.at[q, to], grad_r.at[q, mp], grad_ss.at[q, to], grad_rs.at[q, mp], (g, dp, to)
        )

    def grad_in(q, t):
        fr = lax.rem(mp + t, 16)
        return rc(
            grad_r.at[q, fr], grad_r.at[q, fr], grad_ss.at[q, fr], grad_rs.at[q, fr], (g, dp, fr)
        )

    for cc in range(2):
        far_in(cc).wait_recv()
        swap_out(cc).start()
    pow_cp.wait_recv()
    divs = []
    for j in range(2):
        power = (pow_s[j : j + 1, :] + pow_r[j : j + 1, :]) / KV + power_eps
        length = len_row[0:1, pl.ds(pl.multiple_of((mp % 4) * 256 + j * 128, 128), 128)]
        divs.append(to_col(length * power))
    for q in range(NQ):
        for j in range(2):
            rows = slice(j * 128, (j + 1) * 128)
            wall[q, dp, rows, :] = (total[rows, q * QW : q * QW + QW] / divs[j]).astype(BF16)
        for e in (1, 3, 2):
            wal_out(q, e).start()
        wac_out(q, 0).start()

    def accumulate(q, slot):
        grad[q % 2] += jnp.dot(nturn[slot], wall[q, slot], preferred_element_type=F32)

    def begin(q):
        grad[q % 2] = jnp.zeros((512, QW), F32)
        accumulate(q, dp)
        wac_in(q, 0).wait_recv()
        accumulate(q, x * 2 + 1 - c)

    begin(0)
    for q in range(NQ):
        for e in (1, 3):
            wal_in(q, e).wait_recv()
            wac_out(q, e).start()
        accumulate(q, xp(-1) * 2 + c)
        accumulate(q, xp(-3) * 2 + c)
        if q == 0:
            for cc in range(2):
                swap_in(cc).wait_recv()
                turn(xp(2) * 2 + cc)
        wal_in(q, 2).wait_recv()
        wac_out(q, 2).start()
        accumulate(q, xp(-2) * 2 + c)
        for e in (1, 3):
            wac_in(q, e).wait_recv()
            accumulate(q, xp(-e) * 2 + 1 - c)
        if q + 1 < NQ:
            begin(q + 1)
        wac_in(q, 2).wait_recv()
        accumulate(q, xp(-2) * 2 + 1 - c)
        for b in range(16):
            grad_s[q, b] = grad[q % 2, b * 32 : (b + 1) * 32, :].astype(BF16)
        for t in range(1, 16):
            grad_out(q, t).start()
        out_ref[:, q * QW : q * QW + QW] = grad[q % 2, pl.ds(pl.multiple_of(mp * 32, 32), 32), :]

    for q in range(NQ):
        for t in range(1, 16):
            grad_in(q, t).wait_recv()
        acc = out_ref[:, q * QW : q * QW + QW]
        for t in range(1, 16):
            acc = acc + grad_r[q, lax.rem(mp + t, 16)].astype(F32)
        out_ref[:, q * QW : q * QW + QW] = acc

    val_cp.wait_send()
    for e in range(4):
        if e > 0:
            vx_out(e).wait_send()
        vc_out(e).wait_send()
    gain_cp.wait_send()
    w_far.wait_send()
    pow_cp.wait_send()
    for i in range(8):
        hid_out[i].wait_send()
        fwd_out[i].wait_send()
    for d in NEAR:
        wz_out(0, d).wait_send()
        wz_out(1, d).wait_send()
    for s in range(4):
        for u in range(2):
            ring_cp(0, s, u).wait_send()
            ring_cp(1, s, u).wait_send()
    for way in range(2):
        wx_out(way, 0).wait_send()
        wx_out(way, 1).wait_send()
        wx_fw(way).wait_send()
    for e in range(4):
        wc_out(e).wait_send()
        for q in range(NQ):
            wac_out(q, e).wait_send()
    nrm_out(x, 1 - c).wait_send()
    for cc in range(2):
        swap_out(cc).wait_send()
    for e in range(1, 4):
        for q in range(NQ):
            wal_out(q, e).wait_send()
        for cc in range(2):
            (nrm_out(xp(e), cc) if e != 2 else far_out(cc)).wait_send()
    for d in range(1, 8):
        sq_out(d).wait_send()
    for q in range(NQ):
        for t in range(1, 16):
            grad_out(q, t).wait_send()


def per_device(
    teacher_hidden,
    teacher_gain,
    teacher_value,
    student_hidden,
    student_gain,
    student_value,
    segment_ids,
):
    vmem = pl.BlockSpec(memory_space=pltpu.VMEM)
    dma = pltpu.SemaphoreType.DMA
    return pl.pallas_call(
        kernel,
        out_shape=jax.ShapeDtypeStruct((32, 512), F32),
        in_specs=[pl.BlockSpec(memory_space=pl.ANY)] + [vmem] * 6,
        out_specs=vmem,
        scratch_shapes=[
            pltpu.VMEM((2048, 512), BF16),
            pltpu.VMEM((2048, 512), BF16),
            pltpu.VMEM((512, 512), BF16),
            pltpu.VMEM((512,), BF16),
            pltpu.VMEM((8, 256, 512), BF16),
            pltpu.VMEM((8, 256, 512), BF16),
            pltpu.VMEM((8, 512, 256), BF16),
            pltpu.VMEM((8, 2, 256, 512), BF16),
            pltpu.VMEM((2, 4, 256, 512), BF16),
            pltpu.VMEM((2, 4, 256, 512), BF16),
            pltpu.VMEM((8, 8, 128), F32),
            pltpu.VMEM((8, 8, 128), F32),
            pltpu.VMEM((256, 512), F32),
            pltpu.VMEM((256, 512), F32),
            pltpu.VMEM((8, 128), F32),
            pltpu.VMEM((8, 128), F32),
            pltpu.VMEM((8, 1024), F32),
            pltpu.VMEM((NQ, 8, 256, QW), BF16),
            pltpu.VMEM((2, 512, QW), F32),
            pltpu.VMEM((NQ, 16, 32, QW), BF16),
            pltpu.VMEM((NQ, 16, 32, QW), BF16),
            dma((3,)),
            dma((8,)),
            dma((8,)),
            dma((8,)),
            dma((8,)),
            dma((5,)),
            dma((5,)),
            dma((4,)),
            dma((4,)),
            dma((4,)),
            dma((4,)),
            dma((2, 8)),
            dma((2, 8)),
            dma((3, 2)),
            dma((3, 2)),
            dma((4,)),
            dma((4,)),
            dma((8,)),
            dma((8,)),
            dma((2,)),
            dma((2,)),
            dma((2, 4, 2)),
            dma((2, 4, 2)),
            dma((8,)),
            dma((8,)),
            dma((NQ, 3)),
            dma((NQ, 3)),
            dma((NQ, 4)),
            dma((NQ, 4)),
            dma((NQ, 16)),
            dma((NQ, 16)),
        ],
        compiler_params=pltpu.CompilerParams(
            collective_id=0, has_side_effects=True, vmem_limit_bytes=56 * 1024 * 1024
        ),
    )(
        teacher_hidden,
        teacher_gain,
        teacher_value,
        student_hidden,
        student_gain,
        student_value,
        segment_ids,
    )


def solution(mesh):
    return jax.shard_map(
        per_device,
        mesh=mesh,
        in_specs=(
            P("dp", "mp"),
            P("mp"),
            P("mp", "grp"),
            P(("dp", "mp"), None),
            P(),
            P(("dp", "mp"), "grp"),
            P("dp", None),
        ),
        out_specs=P(("dp", "mp"), "grp"),
        check_vma=False,
    )
```

```python
import jax
import jax.numpy as jnp
from jax import lax
from jax.experimental import pallas as pl
from jax.experimental.pallas import tpu as pltpu
from jax.sharding import PartitionSpec as P

DT = 8192
DS = 4096
KV = 1024
NSEG = 8
MESH = pl.DeviceIdType.MESH
F32 = jnp.float32
BF16 = jnp.bfloat16

norm_eps = 1e-05
power_eps = 1e-06

ORDER = (4, 3, -3, 2, -2, 1, -1, 0)
NHID = 2
NQ = 4
QW = 512 // NQ
NEAR = (4, 3, -3, 2, -2, 1, -1)


def kernel(
    hid_ref,
    gain_in,
    val_in,
    stu_in,
    sgain_in,
    wsh_ref,
    seg_in,
    out_ref,
    gain_ref,
    val_ref,
    stu_ref,
    sgain_ref,
    seg_ref,
    own,
    oth,
    valo,
    gaino,
    nrm,
    nall,
    nturn,
    wgt,
    ring_s,
    ring_r,
    sq_s,
    sq_r,
    states,
    total,
    pow_s,
    pow_r,
    len_row,
    wall,
    grad,
    grad_s,
    grad_r,
    loc_sem,
    hid_ss,
    hid_rs,
    fwd_ss,
    fwd_rs,
    misc_ss,
    misc_rs,
    vx_ss,
    vx_rs,
    vc_ss,
    vc_rs,
    wz_ss,
    wz_rs,
    wx_ss,
    wx_rs,
    wc_ss,
    wc_rs,
    nrm_ss,
    nrm_rs,
    swap_ss,
    swap_rs,
    pow_ss,
    pow_rs,
    ring_ss,
    ring_rs,
    sq_ss,
    sq_rs,
    wal_ss,
    wal_rs,
    wac_ss,
    wac_rs,
    grad_ss,
    grad_rs,
):
    g = lax.axis_index("grp")
    dp = lax.axis_index("dp")
    mp = lax.axis_index("mp")
    x, c = dp // 2, dp % 2
    h, z = mp // 8, mp % 8

    def at(grp=None, xx=None, cc=None, hh=None, zz=None):
        return (
            g if grp is None else grp,
            (x if xx is None else xx) * 2 + (c if cc is None else cc),
            (h if hh is None else hh) * 8 + (z if zz is None else zz),
        )

    def rc(src, dst, ss, rs, dev):
        return pltpu.make_async_remote_copy(
            src_ref=src, dst_ref=dst, send_sem=ss, recv_sem=rs, device_id=dev, device_id_type=MESH
        )

    zp = lambda d: lax.rem(z + d + 8, 8)
    xp = lambda e: lax.rem(x + e + 4, 4)
    grp_dev = at(grp=1 - g)
    cross_dev = at(grp=1 - g, hh=1 - h)
    far_dev = at(hh=1 - h)
    core_dev = at(cc=1 - c)

    own_cp = pltpu.make_async_copy(
        hid_ref.at[pl.ds(pl.multiple_of(h * 2048, 2048), 2048), :], own, loc_sem.at[0]
    )
    w_cp = pltpu.make_async_copy(
        wsh_ref, wgt.at[dp, h, pl.ds(pl.multiple_of(z * 32, 32), 32), :], loc_sem.at[1]
    )
    w_cp.start()
    gain_ld = pltpu.make_async_copy(gain_in, gain_ref, loc_sem.at[3])
    val_ld = pltpu.make_async_copy(val_in, val_ref, loc_sem.at[4])
    stu_ld = pltpu.make_async_copy(stu_in, stu_ref, loc_sem.at[5])
    sgain_ld = pltpu.make_async_copy(sgain_in, sgain_ref, loc_sem.at[6])
    seg_ld = pltpu.make_async_copy(seg_in, seg_ref, loc_sem.at[7])
    for ld in (stu_ld, sgain_ld, seg_ld, gain_ld, val_ld):
        ld.start()
    own_cp.start()

    barrier = pltpu.get_barrier_semaphore()
    count = 0
    for d in range(1, 8):
        pl.semaphore_signal(barrier, inc=1, device_id=at(zz=zp(d)), device_id_type=MESH)
        count += 1
    for d in range(8):
        pl.semaphore_signal(barrier, inc=1, device_id=at(hh=1 - h, zz=zp(d)), device_id_type=MESH)
        count += 1
    for e in range(1, 4):
        for cc in range(2):
            pl.semaphore_signal(
                barrier, inc=1, device_id=at(xx=xp(e), cc=cc), device_id_type=MESH
            )
            count += 1
    for dev in (grp_dev, cross_dev, core_dev):
        pl.semaphore_signal(barrier, inc=1, device_id=dev, device_id_type=MESH)
        count += 1

    pl.semaphore_wait(barrier, count)

    def wz_piece(hh, d):
        return wgt.at[dp, hh, pl.ds(pl.multiple_of(zp(d) * 32, 32), 32), :]

    def wz_out(b, d):
        src = wsh_ref if b == 0 else wz_piece(1 - h, 0)
        dst = wz_piece(h if b == 0 else 1 - h, 0)
        return rc(src, dst, wz_ss.at[b, zp(d)], wz_rs.at[b, z], at(zz=zp(d)))

    def wz_in(b, d):
        piece = wz_piece(h if b == 0 else 1 - h, d)
        return rc(piece, piece, wz_ss.at[b, zp(d)], wz_rs.at[b, zp(d)], at(zz=zp(d)))

    wrow = lambda hh: wz_piece(hh, 0)
    w_far = rc(wsh_ref, wrow(h), misc_ss.at[3], misc_rs.at[3], far_dev)
    w_far_in = rc(wsh_ref, wrow(1 - h), misc_ss.at[3], misc_rs.at[3], far_dev)
    w_far.start()
    def vblock(xx, cc):
        return valo.at[pl.ds(pl.multiple_of((xx * 2 + cc) * 64, 64), 64), :]

    val_cp = rc(
        val_in.at[pl.ds(pl.multiple_of(dp * 64, 64), 64), :],
        vblock(x, c),
        misc_ss.at[0],
        misc_rs.at[0],
        far_dev,
    )
    val_cp.start()

    def vx_out(e):
        b = vblock(x, c)
        return rc(b, b, vx_ss.at[e], vx_rs.at[e], at(xx=xp(e)))

    def vx_in(e):
        b = vblock(xp(-e), c)
        return rc(b, b, vx_ss.at[e], vx_rs.at[e], at(xx=xp(e)))

    def vc_out(e):
        b = vblock(xp(-e), c)
        return rc(b, b, vc_ss.at[e], vc_rs.at[e], core_dev)

    def vc_in(e):
        b = vblock(xp(-e), 1 - c)
        return rc(b, b, vc_ss.at[e], vc_rs.at[e], core_dev)

    gain_cp = rc(gain_in, gaino, misc_ss.at[2], misc_rs.at[2], cross_dev)
    gain_cp.start()

    def hid_rows(hh, i, j):
        return pl.ds(pl.multiple_of(hh * 2048 + zp(ORDER[i]) * 256 + j * 128, 128), 128)

    def loc_rows(i, j):
        return pl.ds(pl.multiple_of(zp(ORDER[i]) * 256 + j * 128, 128), 128)

    hid_out, hid_in, fwd_out, fwd_in = [], [], [], []
    for i in range(8):
        hid_out.append(
            rc(
                hid_ref.at[hid_rows(1 - h, i, 1 - g), :],
                oth.at[loc_rows(i, 1 - g), :],
                hid_ss.at[i],
                hid_rs.at[i],
                cross_dev,
            )
        )
        mine = oth.at[loc_rows(i, g), :]
        theirs = oth.at[loc_rows(i, 1 - g), :]
        hid_in.append(rc(mine, mine, hid_ss.at[i], hid_rs.at[i], cross_dev))
        fwd_out.append(rc(mine, mine, fwd_ss.at[i], fwd_rs.at[i], grp_dev))
        fwd_in.append(rc(theirs, theirs, fwd_ss.at[i], fwd_rs.at[i], grp_dev))
    for d in NEAR:
        wz_out(0, d).start()
    for i in range(NHID):
        hid_out[i].start()

    def nrm_out(xx, cc, part):
        to, rows = xx * 2 + cc, pl.ds(part * 128, 128)
        return rc(
            nrm.at[to, rows, :],
            nall.at[dp, rows, :],
            nrm_ss.at[to, part],
            nrm_rs.at[dp, part],
            at(xx=xx, cc=cc),
        )

    def nrm_wait(xx, cc):
        fr = xx * 2 + cc
        for part in range(2):
            b = nall.at[fr, pl.ds(part * 128, 128), :]
            rc(b, b, nrm_ss.at[fr, part], nrm_rs.at[fr, part], at(xx=xx, cc=cc)).wait_recv()

    grows = lambda gg: pl.ds(pl.multiple_of(gg * 128, 128), 128)

    def far_out(cc):
        to = xp(2) * 2 + cc
        return rc(
            nrm.at[to, grows(g), :],
            nall.at[dp, grows(g), :],
            nrm_ss.at[to, 0],
            nrm_rs.at[dp, 0],
            at(xx=xp(2), cc=cc),
        )

    def far_in(cc):
        b = nall.at[xp(2) * 2 + cc, grows(g), :]
        return rc(b, b, nrm_ss.at[xp(2) * 2 + cc, 0], nrm_rs.at[xp(2) * 2 + cc, 0], grp_dev)

    def swap_out(cc):
        b = nall.at[xp(2) * 2 + cc, grows(g), :]
        return rc(b, b, swap_ss.at[cc], swap_rs.at[cc], grp_dev)

    def swap_in(cc):
        b = nall.at[xp(2) * 2 + cc, grows(1 - g), :]
        return rc(b, b, swap_ss.at[cc], swap_rs.at[cc], grp_dev)

    stu_ld.wait()
    sgain_ld.wait()
    sgain = sgain_ref[...].astype(F32).reshape(1, DS)

    @pl.loop(0, 8)
    def _(i):
        rows = pl.ds(pl.multiple_of(i * 32, 32), 32)
        wide = stu_ref[rows, :].astype(F32)
        scale = lax.rsqrt(jnp.sum(wide * wide, axis=1, keepdims=True) / DS + norm_eps)
        done = (wide * scale * sgain).astype(BF16)
        for b in range(8):
            nrm[b, rows, :] = done[:, b * 512 : (b + 1) * 512]

    nrm_own = pltpu.make_async_copy(nrm.at[dp], nall.at[dp], loc_sem.at[2])
    nrm_own.start()

    seg_ld.wait()
    seg = seg_ref[pl.ds(mp // 4, 1), :]
    lens = jnp.zeros((1, 1024), F32)
    for s in range(NSEG):
        hit = (seg == s).astype(F32)
        lens = lens + hit * jnp.sum(hit, axis=1, keepdims=True)
    len_row[0:1, :] = lens

    eye = lax.broadcasted_iota(jnp.int32, (128, 128), 0) == lax.broadcasted_iota(
        jnp.int32, (128, 128), 1
    )

    def to_row(col):
        return jnp.sum(jnp.where(eye, col, 0.0), axis=0, keepdims=True)

    def to_col(row):
        return jnp.sum(jnp.where(eye, row, 0.0), axis=1, keepdims=True)

    for e in (1, 3):
        nrm_out(xp(e), c, 0).start()
    for part in range(2):
        nrm_out(x, 1 - c, part).start()

    def wblock(xx, cc=None):
        return wgt.at[xx * 2 + (c if cc is None else cc)]

    def wx_dev(way):
        return at(xx=xp(1 if way == 0 else -1))

    def wx_out(way, part):
        b = wblock(x).at[way if part == 0 else 1 - way]
        return rc(b, b, wx_ss.at[part, way], wx_rs.at[part, way], wx_dev(way))

    def wx_in(way, part):
        b = wblock(xp(-1 if way == 0 else 1)).at[way if part == 0 else 1 - way]
        return rc(b, b, wx_ss.at[part, way], wx_rs.at[part, way], wx_dev(way))

    def wx_fw(way):
        b = wblock(xp(-1 if way == 0 else 1)).at[way]
        return rc(b, b, wx_ss.at[2, way], wx_rs.at[2, way], wx_dev(way))

    def wx_fin(way):
        b = wblock(xp(2)).at[way]
        return rc(b, b, wx_ss.at[2, way], wx_rs.at[2, way], wx_dev(way))

    def wc_out(e):
        b = wblock(xp(e))
        return rc(b, b, wc_ss.at[e], wc_rs.at[e], core_dev)

    def wc_in(e):
        b = wblock(xp(e), 1 - c)
        return rc(b, b, wc_ss.at[e], wc_rs.at[e], core_dev)

    jrow = lambda u: g if u == 0 else 1 - g
    urows = lambda j: pl.ds(pl.multiple_of(j * 128, 128), 128)

    def ring_cp(way, s, u):
        rows = urows(jrow(u))
        cols = pl.ds(way * 256, 256) if s == 0 else pl.ds(0, 512)
        dev = at(zz=zp(1 if way == 0 else -1))
        return rc(
            ring_s.at[way, s, rows, cols],
            ring_r.at[way, s, rows, cols],
            ring_ss.at[way, s, u],
            ring_rs.at[way, s, u],
            dev,
        )

    def sq_out(d):
        return rc(sq_s.at[zp(d)], sq_r.at[z], sq_ss.at[zp(d)], sq_rs.at[z], at(zz=zp(d)))

    def sq_in(d):
        return rc(sq_r.at[zp(d)], sq_r.at[zp(d)], sq_ss.at[zp(d)], sq_rs.at[zp(d)], at(zz=zp(d)))

    def sub(i, u):
        d = ORDER[i]
        k = zp(d)
        j = jrow(u)
        if u == 1:
            fwd_in[i].wait_recv()
        if d == 0:
            ring_cp(0, 3, u).wait_recv()
            ring_cp(1, 3, u).wait_recv()
        elif d != 4:
            ring_cp(0 if d > 0 else 1, 3 - abs(d), u).wait_recv()
        rows = pl.ds(pl.multiple_of(k * 256 + j * 128, 128), 128)
        brows = urows(j)
        h1 = own[rows, :].astype(F32)
        h2 = oth[rows, :].astype(F32)
        tgain = gain_ref[...].astype(F32).reshape(1, 512)
        tgaino = gaino[...].astype(F32).reshape(1, 512)
        acc = jnp.dot((h1 * tgain).astype(BF16), val_ref[...], preferred_element_type=F32)
        acc += jnp.dot((h2 * tgaino).astype(BF16), valo[...], preferred_element_type=F32)
        sq = jnp.sum(h1 * h1 + h2 * h2, axis=1, keepdims=True)
        sq_s[k, pl.ds(j, 1), :] = to_row(sq)
        if u == 1 and d != 0:
            sq_out(d).start()
        if d == 4:
            ring_s[0, 0, brows, 0:256] = acc[:, 0:256].astype(BF16)
            ring_s[1, 0, brows, 256:512] = acc[:, 256:512].astype(BF16)
            ring_cp(0, 0, u).start()
            ring_cp(1, 0, u).start()
        elif d == 0:
            total[brows, :] = (
                acc + ring_r[0, 3, brows, :].astype(F32) + ring_r[1, 3, brows, :].astype(F32)
            )
        else:
            way, s = (0 if d > 0 else 1), 4 - abs(d)
            if s == 1:
                cols = slice(way * 256, way * 256 + 256)
                rest = slice((1 - way) * 256, (1 - way) * 256 + 256)
                ring_s[way, s, brows, cols] = (
                    acc[:, cols] + ring_r[way, 0, brows, cols].astype(F32)
                ).astype(BF16)
                ring_s[way, s, brows, rest] = acc[:, rest].astype(BF16)
            else:
                ring_s[way, s, brows, :] = (
                    acc + ring_r[way, s - 1, brows, :].astype(F32)
                ).astype(BF16)
            ring_cp(way, s, u).start()

    def turn(slot):
        nturn[slot] = nall[slot].T

    def take(i):
        hid_in[i].wait_recv()
        fwd_out[i].start()

    def add_states(blocks):
        part = None
        for b in blocks:
            for hh in range(2):
                t = jnp.dot(
                    nrm[b, :, hh * 256 : hh * 256 + 256], wgt[b, hh], preferred_element_type=F32
                )
                part = t if part is None else part + t
        states[...] += part

    states[...] = jnp.zeros_like(states)
    val_cp.wait_recv()
    for e in (2, 1, 3):
        vx_out(e).start()
    vc_out(0).start()
    for e in (1, 3):
        nrm_out(xp(e), c, 1).start()
    for part in range(2):
        for e in (1, 3):
            nrm_out(xp(e), 1 - c, part).start()
    for i in range(NHID, 8):
        hid_out[i].start()
    w_far_in.wait_recv()
    for d in NEAR:
        wz_out(1, d).start()
    take(0)
    for e in (1, 3, 2):
        vx_in(e).wait_recv()
        vc_out(e).start()
    own_cp.wait()
    w_cp.wait()
    gain_ld.wait()
    val_ld.wait()
    gain_cp.wait_recv()
    take(1)
    for e in range(4):
        vc_in(e).wait_recv()
    sub(0, 0)
    sub(0, 1)
    for b in range(2):
        for d in NEAR:
            wz_in(b, d).wait_recv()
    for part in range(2):
        for way in range(2):
            wx_out(way, part).start()
    wc_out(0).start()
    take(2)
    sub(1, 0)
    sub(2, 0)
    take(3)
    nrm_own.wait()
    turn(dp)
    nrm_wait(x, 1 - c)
    turn(x * 2 + 1 - c)
    sub(1, 1)
    sub(2, 1)
    take(4)
    sub(3, 0)
    sub(4, 0)
    take(5)
    sub(3, 1)
    sub(4, 1)
    for way in range(2):
        wx_in(way, 0).wait_recv()
        wx_fw(way).start()
    for cc in range(2):
        nrm_wait(xp(1), cc)
        turn(xp(1) * 2 + cc)
    take(6)
    wc_in(0).wait_recv()
    add_states((dp, x * 2 + 1 - c))
    sub(5, 0)
    sub(6, 0)
    take(7)
    sub(5, 1)
    sub(6, 1)
    for cc in range(2):
        far_out(cc).start()
    for way in range(2):
        wx_in(way, 1).wait_recv()
    wc_out(1).start()
    wc_out(3).start()
    add_states((xp(1) * 2 + c, xp(-1) * 2 + c))
    for cc in range(2):
        nrm_wait(xp(3), cc)
        turn(xp(3) * 2 + cc)
    def power(j):
        rows = urows(j)
        row = sq_s[z, pl.ds(j, 1), :]
        for d in range(1, 8):
            row = row + sq_r[zp(d), pl.ds(j, 1), :]
        target = total[rows, :] * lax.rsqrt(to_col(row) / DT + norm_eps)
        total[rows, :] = target
        pow_s[j, 0:1, :] = to_row(jnp.sum(target * target, axis=1, keepdims=True))
        pow_cp(j).start()

    def pow_cp(j):
        return rc(pow_s.at[j], pow_r.at[j], pow_ss.at[j], pow_rs.at[j], grp_dev)

    sub(7, 0)
    for d in range(1, 8):
        sq_in(d).wait_recv()
    power(g)
    wx_fin(0).wait_recv()
    wx_fin(1).wait_recv()
    wc_out(2).start()
    sub(7, 1)
    power(1 - g)
    wc_in(1).wait_recv()
    wc_in(3).wait_recv()
    add_states((xp(1) * 2 + 1 - c, xp(-1) * 2 + 1 - c))
    far_in(c).wait_recv()
    swap_out(c).start()
    wc_in(2).wait_recv()
    add_states((xp(2) * 2, xp(2) * 2 + 1))

    def wal_out(q, e, u):
        b = wall.at[q, dp, urows(u), :]
        return rc(b, b, wal_ss.at[q, e - 1, u], wal_rs.at[q, e - 1, u], at(xx=xp(e)))

    def wal_in(q, e, u):
        b = wall.at[q, xp(-e) * 2 + c, urows(u), :]
        return rc(b, b, wal_ss.at[q, e - 1, u], wal_rs.at[q, e - 1, u], at(xx=xp(e)))

    def wac_out(q, e, u):
        b = wall.at[q, xp(-e) * 2 + c, urows(u), :]
        return rc(b, b, wac_ss.at[q, e, u], wac_rs.at[q, e, u], core_dev)

    def wac_wait(q, e):
        for u in range(2):
            b = wall.at[q, xp(-e) * 2 + 1 - c, urows(u), :]
            rc(b, b, wac_ss.at[q, e, u], wac_rs.at[q, e, u], core_dev).wait_recv()

    def pass_on(q, e):
        for j in (1 - g, g):
            wal_in(q, e, j).wait_recv()
            wac_out(q, e, j).start()

    def grad_out(q, t):
        to = lax.rem(mp + t, 16)
        return rc(
            grad_s.at[q, to], grad_r.at[q, mp], grad_ss.at[q, to], grad_rs.at[q, mp], (g, dp, to)
        )

    def grad_in(q, t):
        fr = lax.rem(mp + t, 16)
        return rc(
            grad_r.at[q, fr], grad_r.at[q, fr], grad_ss.at[q, fr], grad_rs.at[q, fr], (g, dp, fr)
        )

    def weigh(q, j, div):
        rows, cols = urows(j), slice(q * QW, q * QW + QW)
        wall[q, dp, rows, :] = ((states[rows, cols] - total[rows, cols]) / div).astype(BF16)
        for e in (1, 3, 2):
            wal_out(q, e, j).start()
        wac_out(q, 0, j).start()

    divs = []
    for j in (1 - g, g):
        pow_cp(j).wait_recv()
        power_j = (pow_s[j, 0:1, :] + pow_r[j, 0:1, :]) / KV + power_eps
        start = pl.multiple_of((mp % 4) * 256 + j * 128, 128)
        divs.append(to_col(len_row[0:1, pl.ds(start, 128)] * power_j))
        weigh(0, j, divs[-1])
    for q in range(1, NQ):
        for j, div in zip((1 - g, g), divs):
            weigh(q, j, div)
    far_in(1 - c).wait_recv()
    swap_out(1 - c).start()

    def accumulate(q, slot):
        grad[q % 2] += jnp.dot(nturn[slot], wall[q, slot], preferred_element_type=F32)

    def begin(q):
        grad[q % 2] = jnp.zeros((512, QW), F32)
        accumulate(q, dp)
        wac_wait(q, 0)
        accumulate(q, x * 2 + 1 - c)

    begin(0)
    for q in range(NQ):
        for e in (1, 3):
            pass_on(q, e)
        accumulate(q, xp(-1) * 2 + c)
        accumulate(q, xp(-3) * 2 + c)
        if q == 0:
            for cc in range(2):
                swap_in(cc).wait_recv()
                turn(xp(2) * 2 + cc)
        pass_on(q, 2)
        accumulate(q, xp(-2) * 2 + c)
        for e in (1, 3):
            wac_wait(q, e)
            accumulate(q, xp(-e) * 2 + 1 - c)
        if q + 1 < NQ:
            begin(q + 1)
        wac_wait(q, 2)
        accumulate(q, xp(-2) * 2 + 1 - c)
        for b in range(16):
            grad_s[q, b] = grad[q % 2, b * 32 : (b + 1) * 32, :].astype(BF16)
        for t in range(1, 16):
            grad_out(q, t).start()
        out_ref[:, q * QW : q * QW + QW] = grad[q % 2, pl.ds(pl.multiple_of(mp * 32, 32), 32), :]

    for q in range(NQ):
        for t in range(1, 16):
            grad_in(q, t).wait_recv()
        acc = out_ref[:, q * QW : q * QW + QW]
        for t in range(1, 16):
            acc = acc + grad_r[q, lax.rem(mp + t, 16)].astype(F32)
        out_ref[:, q * QW : q * QW + QW] = acc

    val_cp.wait_send()
    for e in range(4):
        if e > 0:
            vx_out(e).wait_send()
        vc_out(e).wait_send()
    gain_cp.wait_send()
    w_far.wait_send()
    for u in range(2):
        pow_cp(u).wait_send()
    for i in range(8):
        hid_out[i].wait_send()
        fwd_out[i].wait_send()
    for d in NEAR:
        wz_out(0, d).wait_send()
        wz_out(1, d).wait_send()
    for s in range(4):
        for u in range(2):
            ring_cp(0, s, u).wait_send()
            ring_cp(1, s, u).wait_send()
    for way in range(2):
        wx_out(way, 0).wait_send()
        wx_out(way, 1).wait_send()
        wx_fw(way).wait_send()
    for e in range(4):
        wc_out(e).wait_send()
        for q in range(NQ):
            for u in range(2):
                wac_out(q, e, u).wait_send()
    nrm_out(x, 1 - c, 0).wait_send()
    nrm_out(x, 1 - c, 1).wait_send()
    for cc in range(2):
        swap_out(cc).wait_send()
    for e in range(1, 4):
        for q in range(NQ):
            for u in range(2):
                wal_out(q, e, u).wait_send()
        for cc in range(2):
            if e == 2:
                far_out(cc).wait_send()
            else:
                nrm_out(xp(e), cc, 0).wait_send()
                nrm_out(xp(e), cc, 1).wait_send()
    for d in range(1, 8):
        sq_out(d).wait_send()
    for q in range(NQ):
        for t in range(1, 16):
            grad_out(q, t).wait_send()


def per_device(
    teacher_hidden,
    teacher_gain,
    teacher_value,
    student_hidden,
    student_gain,
    student_value,
    segment_ids,
):
    vmem = pl.BlockSpec(memory_space=pltpu.VMEM)
    dma = pltpu.SemaphoreType.DMA
    return pl.pallas_call(
        kernel,
        out_shape=jax.ShapeDtypeStruct((32, 512), F32),
        in_specs=[pl.BlockSpec(memory_space=pl.ANY)] * 7,
        out_specs=vmem,
        scratch_shapes=[
            pltpu.VMEM((512,), BF16),
            pltpu.VMEM((512, 512), BF16),
            pltpu.VMEM((256, 4096), BF16),
            pltpu.VMEM((4096,), BF16),
            pltpu.VMEM((4, 1024), jnp.int32),
            pltpu.VMEM((2048, 512), BF16),
            pltpu.VMEM((2048, 512), BF16),
            pltpu.VMEM((512, 512), BF16),
            pltpu.VMEM((512,), BF16),
            pltpu.VMEM((8, 256, 512), BF16),
            pltpu.VMEM((8, 256, 512), BF16),
            pltpu.VMEM((8, 512, 256), BF16),
            pltpu.VMEM((8, 2, 256, 512), BF16),
            pltpu.VMEM((2, 4, 256, 512), BF16),
            pltpu.VMEM((2, 4, 256, 512), BF16),
            pltpu.VMEM((8, 8, 128), F32),
            pltpu.VMEM((8, 8, 128), F32),
            pltpu.VMEM((256, 512), F32),
            pltpu.VMEM((256, 512), F32),
            pltpu.VMEM((2, 8, 128), F32),
            pltpu.VMEM((2, 8, 128), F32),
            pltpu.VMEM((8, 1024), F32),
            pltpu.VMEM((NQ, 8, 256, QW), BF16),
            pltpu.VMEM((2, 512, QW), F32),
            pltpu.VMEM((NQ, 16, 32, QW), BF16),
            pltpu.VMEM((NQ, 16, 32, QW), BF16),
            dma((8,)),
            dma((8,)),
            dma((8,)),
            dma((8,)),
            dma((8,)),
            dma((5,)),
            dma((5,)),
            dma((4,)),
            dma((4,)),
            dma((4,)),
            dma((4,)),
            dma((2, 8)),
            dma((2, 8)),
            dma((3, 2)),
            dma((3, 2)),
            dma((4,)),
            dma((4,)),
            dma((8, 2)),
            dma((8, 2)),
            dma((2,)),
            dma((2,)),
            dma((2,)),
            dma((2,)),
            dma((2, 4, 2)),
            dma((2, 4, 2)),
            dma((8,)),
            dma((8,)),
            dma((NQ, 3, 2)),
            dma((NQ, 3, 2)),
            dma((NQ, 4, 2)),
            dma((NQ, 4, 2)),
            dma((NQ, 16)),
            dma((NQ, 16)),
        ],
        compiler_params=pltpu.CompilerParams(
            collective_id=0, has_side_effects=True, vmem_limit_bytes=56 * 1024 * 1024
        ),
    )(
        teacher_hidden,
        teacher_gain,
        teacher_value,
        student_hidden,
        student_gain,
        student_value,
        segment_ids,
    )


def solution(mesh):
    return jax.shard_map(
        per_device,
        mesh=mesh,
        in_specs=(
            P("dp", "mp"),
            P("mp"),
            P("mp", "grp"),
            P(("dp", "mp"), None),
            P(),
            P(("dp", "mp"), "grp"),
            P("dp", None),
        ),
        out_specs=P(("dp", "mp"), "grp"),
        check_vma=False,
    )
```

```python
import jax
import jax.numpy as jnp
from jax import lax
from jax.experimental import pallas as pl
from jax.experimental.pallas import tpu as pltpu
from jax.sharding import PartitionSpec as P

DT = 8192
DS = 4096
KV = 1024
NSEG = 8
MESH = pl.DeviceIdType.MESH
F32 = jnp.float32
BF16 = jnp.bfloat16

norm_eps = 1e-05
power_eps = 1e-06

ORDER = (4, 3, -3, 2, -2, 1, -1, 0)
NHID = 2
NQ = 4
QW = 512 // NQ
NEAR = (4, 3, -3, 2, -2, 1, -1)


def kernel(
    hid_ref,
    gain_in,
    val_in,
    stu_in,
    sgain_in,
    wsh_ref,
    seg_in,
    out_ref,
    gain_ref,
    val_ref,
    stu_ref,
    sgain_ref,
    seg_ref,
    own,
    oth,
    valo,
    gaino,
    nrm,
    nall,
    nturn,
    wgt,
    ring_s,
    ring_r,
    sq_s,
    sq_r,
    states,
    total,
    pow_s,
    pow_r,
    len_row,
    wall,
    grad,
    grad_s,
    grad_r,
    loc_sem,
    hid_ss,
    hid_rs,
    fwd_ss,
    fwd_rs,
    misc_ss,
    misc_rs,
    vx_ss,
    vx_rs,
    vc_ss,
    vc_rs,
    wz_ss,
    wz_rs,
    wx_ss,
    wx_rs,
    wc_ss,
    wc_rs,
    nrm_ss,
    nrm_rs,
    swap_ss,
    swap_rs,
    pow_ss,
    pow_rs,
    ring_ss,
    ring_rs,
    sq_ss,
    sq_rs,
    wal_ss,
    wal_rs,
    wac_ss,
    wac_rs,
    grad_ss,
    grad_rs,
):
    g = lax.axis_index("grp")
    dp = lax.axis_index("dp")
    mp = lax.axis_index("mp")
    x, c = dp // 2, dp % 2
    h, z = mp // 8, mp % 8

    def at(grp=None, xx=None, cc=None, hh=None, zz=None):
        return (
            g if grp is None else grp,
            (x if xx is None else xx) * 2 + (c if cc is None else cc),
            (h if hh is None else hh) * 8 + (z if zz is None else zz),
        )

    def rc(src, dst, ss, rs, dev):
        return pltpu.make_async_remote_copy(
            src_ref=src, dst_ref=dst, send_sem=ss, recv_sem=rs, device_id=dev, device_id_type=MESH
        )

    zp = lambda d: lax.rem(z + d + 8, 8)
    xp = lambda e: lax.rem(x + e + 4, 4)
    grp_dev = at(grp=1 - g)
    cross_dev = at(grp=1 - g, hh=1 - h)
    far_dev = at(hh=1 - h)
    core_dev = at(cc=1 - c)

    own_cp = pltpu.make_async_copy(
        hid_ref.at[pl.ds(pl.multiple_of(h * 2048, 2048), 2048), :], own, loc_sem.at[0]
    )
    w_cp = pltpu.make_async_copy(
        wsh_ref, wgt.at[dp, h, pl.ds(pl.multiple_of(z * 32, 32), 32), :], loc_sem.at[1]
    )
    w_cp.start()
    gain_ld = pltpu.make_async_copy(gain_in, gain_ref, loc_sem.at[3])
    val_ld = pltpu.make_async_copy(val_in, val_ref, loc_sem.at[4])
    stu_ld = pltpu.make_async_copy(stu_in, stu_ref, loc_sem.at[5])
    sgain_ld = pltpu.make_async_copy(sgain_in, sgain_ref, loc_sem.at[6])
    seg_ld = pltpu.make_async_copy(seg_in, seg_ref, loc_sem.at[7])
    for ld in (stu_ld, sgain_ld, seg_ld, gain_ld, val_ld):
        ld.start()
    own_cp.start()

    barrier = pltpu.get_barrier_semaphore()
    count = 0
    for d in range(1, 8):
        pl.semaphore_signal(barrier, inc=1, device_id=at(zz=zp(d)), device_id_type=MESH)
        count += 1
    for d in range(8):
        pl.semaphore_signal(barrier, inc=1, device_id=at(hh=1 - h, zz=zp(d)), device_id_type=MESH)
        count += 1
    for e in range(1, 4):
        for cc in range(2):
            pl.semaphore_signal(
                barrier, inc=1, device_id=at(xx=xp(e), cc=cc), device_id_type=MESH
            )
            count += 1
    for dev in (grp_dev, cross_dev, core_dev):
        pl.semaphore_signal(barrier, inc=1, device_id=dev, device_id_type=MESH)
        count += 1

    pl.semaphore_wait(barrier, count)

    def wz_piece(hh, d):
        return wgt.at[dp, hh, pl.ds(pl.multiple_of(zp(d) * 32, 32), 32), :]

    def wz_out(b, d):
        src = wsh_ref if b == 0 else wz_piece(1 - h, 0)
        dst = wz_piece(h if b == 0 else 1 - h, 0)
        return rc(src, dst, wz_ss.at[b, zp(d)], wz_rs.at[b, z], at(zz=zp(d)))

    def wz_in(b, d):
        piece = wz_piece(h if b == 0 else 1 - h, d)
        return rc(piece, piece, wz_ss.at[b, zp(d)], wz_rs.at[b, zp(d)], at(zz=zp(d)))

    wrow = lambda hh: wz_piece(hh, 0)
    w_far = rc(wsh_ref, wrow(h), misc_ss.at[3], misc_rs.at[3], far_dev)
    w_far_in = rc(wsh_ref, wrow(1 - h), misc_ss.at[3], misc_rs.at[3], far_dev)
    w_far.start()
    def vblock(xx, cc):
        return valo.at[pl.ds(pl.multiple_of((xx * 2 + cc) * 64, 64), 64), :]

    val_cp = rc(
        val_in.at[pl.ds(pl.multiple_of(dp * 64, 64), 64), :],
        vblock(x, c),
        misc_ss.at[0],
        misc_rs.at[0],
        far_dev,
    )
    val_cp.start()

    def vx_out(e):
        b = vblock(x, c)
        return rc(b, b, vx_ss.at[e], vx_rs.at[e], at(xx=xp(e)))

    def vx_in(e):
        b = vblock(xp(-e), c)
        return rc(b, b, vx_ss.at[e], vx_rs.at[e], at(xx=xp(e)))

    def vc_out(e):
        b = vblock(xp(-e), c)
        return rc(b, b, vc_ss.at[e], vc_rs.at[e], core_dev)

    def vc_in(e):
        b = vblock(xp(-e), 1 - c)
        return rc(b, b, vc_ss.at[e], vc_rs.at[e], core_dev)

    gain_cp = rc(gain_in, gaino, misc_ss.at[2], misc_rs.at[2], cross_dev)
    gain_cp.start()

    def hid_rows(hh, i, j):
        return pl.ds(pl.multiple_of(hh * 2048 + zp(ORDER[i]) * 256 + j * 128, 128), 128)

    def loc_rows(i, j):
        return pl.ds(pl.multiple_of(zp(ORDER[i]) * 256 + j * 128, 128), 128)

    hid_out, hid_in, fwd_out, fwd_in = [], [], [], []
    for i in range(8):
        hid_out.append(
            rc(
                hid_ref.at[hid_rows(1 - h, i, 1 - g), :],
                oth.at[loc_rows(i, 1 - g), :],
                hid_ss.at[i],
                hid_rs.at[i],
                cross_dev,
            )
        )
        mine = oth.at[loc_rows(i, g), :]
        theirs = oth.at[loc_rows(i, 1 - g), :]
        hid_in.append(rc(mine, mine, hid_ss.at[i], hid_rs.at[i], cross_dev))
        fwd_out.append(rc(mine, mine, fwd_ss.at[i], fwd_rs.at[i], grp_dev))
        fwd_in.append(rc(theirs, theirs, fwd_ss.at[i], fwd_rs.at[i], grp_dev))
    for d in NEAR:
        wz_out(0, d).start()
    for i in range(NHID):
        hid_out[i].start()

    def nrm_out(xx, cc, part):
        to, rows = xx * 2 + cc, pl.ds(part * 128, 128)
        return rc(
            nrm.at[to, rows, :],
            nall.at[dp, rows, :],
            nrm_ss.at[to, part],
            nrm_rs.at[dp, part],
            at(xx=xx, cc=cc),
        )

    def nrm_wait(xx, cc):
        fr = xx * 2 + cc
        for part in range(2):
            b = nall.at[fr, pl.ds(part * 128, 128), :]
            rc(b, b, nrm_ss.at[fr, part], nrm_rs.at[fr, part], at(xx=xx, cc=cc)).wait_recv()

    grows = lambda gg: pl.ds(pl.multiple_of(gg * 128, 128), 128)

    def far_out(cc):
        to = xp(2) * 2 + cc
        return rc(
            nrm.at[to, grows(g), :],
            nall.at[dp, grows(g), :],
            nrm_ss.at[to, 0],
            nrm_rs.at[dp, 0],
            at(xx=xp(2), cc=cc),
        )

    def far_in(cc):
        b = nall.at[xp(2) * 2 + cc, grows(g), :]
        return rc(b, b, nrm_ss.at[xp(2) * 2 + cc, 0], nrm_rs.at[xp(2) * 2 + cc, 0], grp_dev)

    def swap_out(cc):
        b = nall.at[xp(2) * 2 + cc, grows(g), :]
        return rc(b, b, swap_ss.at[cc], swap_rs.at[cc], grp_dev)

    def swap_in(cc):
        b = nall.at[xp(2) * 2 + cc, grows(1 - g), :]
        return rc(b, b, swap_ss.at[cc], swap_rs.at[cc], grp_dev)

    stu_ld.wait()
    sgain_ld.wait()
    sgain = sgain_ref[...].astype(F32).reshape(1, DS)

    @pl.loop(0, 8)
    def _(i):
        rows = pl.ds(pl.multiple_of(i * 32, 32), 32)
        wide = stu_ref[rows, :].astype(F32)
        scale = lax.rsqrt(jnp.sum(wide * wide, axis=1, keepdims=True) / DS + norm_eps)
        done = (wide * scale * sgain).astype(BF16)
        for b in range(8):
            nrm[b, rows, :] = done[:, b * 512 : (b + 1) * 512]

    nrm_own = pltpu.make_async_copy(nrm.at[dp], nall.at[dp], loc_sem.at[2])
    nrm_own.start()

    seg_ld.wait()
    seg = seg_ref[pl.ds(mp // 4, 1), :]
    lens = jnp.zeros((1, 1024), F32)
    for s in range(NSEG):
        hit = (seg == s).astype(F32)
        lens = lens + hit * jnp.sum(hit, axis=1, keepdims=True)
    len_row[0:1, :] = lens

    eye = lax.broadcasted_iota(jnp.int32, (128, 128), 0) == lax.broadcasted_iota(
        jnp.int32, (128, 128), 1
    )

    def to_row(col):
        return jnp.sum(jnp.where(eye, col, 0.0), axis=0, keepdims=True)

    def to_col(row):
        return jnp.sum(jnp.where(eye, row, 0.0), axis=1, keepdims=True)

    for e in (1, 3):
        nrm_out(xp(e), c, 0).start()
    for part in range(2):
        nrm_out(x, 1 - c, part).start()

    def wblock(xx, cc=None):
        return wgt.at[xx * 2 + (c if cc is None else cc)]

    def wx_dev(way):
        return at(xx=xp(1 if way == 0 else -1))

    def wx_out(way, part):
        b = wblock(x).at[way if part == 0 else 1 - way]
        return rc(b, b, wx_ss.at[part, way], wx_rs.at[part, way], wx_dev(way))

    def wx_in(way, part):
        b = wblock(xp(-1 if way == 0 else 1)).at[way if part == 0 else 1 - way]
        return rc(b, b, wx_ss.at[part, way], wx_rs.at[part, way], wx_dev(way))

    def wx_fw(way):
        b = wblock(xp(-1 if way == 0 else 1)).at[way]
        return rc(b, b, wx_ss.at[2, way], wx_rs.at[2, way], wx_dev(way))

    def wx_fin(way):
        b = wblock(xp(2)).at[way]
        return rc(b, b, wx_ss.at[2, way], wx_rs.at[2, way], wx_dev(way))

    def wc_out(e):
        b = wblock(xp(e))
        return rc(b, b, wc_ss.at[e], wc_rs.at[e], core_dev)

    def wc_in(e):
        b = wblock(xp(e), 1 - c)
        return rc(b, b, wc_ss.at[e], wc_rs.at[e], core_dev)

    jrow = lambda u: g if u == 0 else 1 - g
    urows = lambda j: pl.ds(pl.multiple_of(j * 128, 128), 128)

    def ring_cp(way, s, u):
        rows = urows(jrow(u))
        cols = pl.ds(way * 256, 256) if s == 0 else pl.ds(0, 512)
        dev = at(zz=zp(1 if way == 0 else -1))
        return rc(
            ring_s.at[way, s, rows, cols],
            ring_r.at[way, s, rows, cols],
            ring_ss.at[way, s, u],
            ring_rs.at[way, s, u],
            dev,
        )

    def sq_out(d):
        return rc(sq_s.at[zp(d)], sq_r.at[z], sq_ss.at[zp(d)], sq_rs.at[z], at(zz=zp(d)))

    def sq_in(d):
        return rc(sq_r.at[zp(d)], sq_r.at[zp(d)], sq_ss.at[zp(d)], sq_rs.at[zp(d)], at(zz=zp(d)))

    def sub(i, u):
        d = ORDER[i]
        k = zp(d)
        j = jrow(u)
        if u == 1:
            fwd_in[i].wait_recv()
        if d == 0:
            ring_cp(0, 3, u).wait_recv()
            ring_cp(1, 3, u).wait_recv()
        elif d != 4:
            ring_cp(0 if d > 0 else 1, 3 - abs(d), u).wait_recv()
        rows = pl.ds(pl.multiple_of(k * 256 + j * 128, 128), 128)
        brows = urows(j)
        h1 = own[rows, :].astype(F32)
        h2 = oth[rows, :].astype(F32)
        tgain = gain_ref[...].astype(F32).reshape(1, 512)
        tgaino = gaino[...].astype(F32).reshape(1, 512)
        acc = jnp.dot((h1 * tgain).astype(BF16), val_ref[...], preferred_element_type=F32)
        acc += jnp.dot((h2 * tgaino).astype(BF16), valo[...], preferred_element_type=F32)
        sq = jnp.sum(h1 * h1 + h2 * h2, axis=1, keepdims=True)
        sq_s[k, pl.ds(j, 1), :] = to_row(sq)
        if u == 1 and d != 0:
            sq_out(d).start()
        if d == 4:
            ring_s[0, 0, brows, 0:256] = acc[:, 0:256].astype(BF16)
            ring_s[1, 0, brows, 256:512] = acc[:, 256:512].astype(BF16)
            ring_cp(0, 0, u).start()
            ring_cp(1, 0, u).start()
        elif d == 0:
            total[brows, :] = (
                acc + ring_r[0, 3, brows, :].astype(F32) + ring_r[1, 3, brows, :].astype(F32)
            )
        else:
            way, s = (0 if d > 0 else 1), 4 - abs(d)
            if s == 1:
                cols = slice(way * 256, way * 256 + 256)
                rest = slice((1 - way) * 256, (1 - way) * 256 + 256)
                ring_s[way, s, brows, cols] = (
                    acc[:, cols] + ring_r[way, 0, brows, cols].astype(F32)
                ).astype(BF16)
                ring_s[way, s, brows, rest] = acc[:, rest].astype(BF16)
            else:
                ring_s[way, s, brows, :] = (
                    acc + ring_r[way, s - 1, brows, :].astype(F32)
                ).astype(BF16)
            ring_cp(way, s, u).start()

    def turn(slot):
        nturn[slot] = nall[slot].T

    def take(i):
        hid_in[i].wait_recv()
        fwd_out[i].start()

    def add_states(blocks):
        part = None
        for b in blocks:
            for hh in range(2):
                t = jnp.dot(
                    nrm[b, :, hh * 256 : hh * 256 + 256], wgt[b, hh], preferred_element_type=F32
                )
                part = t if part is None else part + t
        states[...] += part

    states[...] = jnp.zeros_like(states)
    val_cp.wait_recv()
    for e in (2, 1, 3):
        vx_out(e).start()
    vc_out(0).start()
    for e in (1, 3):
        nrm_out(xp(e), c, 1).start()
    for part in range(2):
        for e in (1, 3):
            nrm_out(xp(e), 1 - c, part).start()
    for i in range(NHID, 8):
        hid_out[i].start()
    w_far_in.wait_recv()
    for d in NEAR:
        wz_out(1, d).start()
    take(0)
    for e in (1, 3, 2):
        vx_in(e).wait_recv()
        vc_out(e).start()
    own_cp.wait()
    w_cp.wait()
    gain_ld.wait()
    val_ld.wait()
    gain_cp.wait_recv()
    take(1)
    for e in range(4):
        vc_in(e).wait_recv()
    sub(0, 0)
    sub(0, 1)
    for b in range(2):
        for d in NEAR:
            wz_in(b, d).wait_recv()
    for part in range(2):
        for way in range(2):
            wx_out(way, part).start()
    wc_out(0).start()
    take(2)
    sub(1, 0)
    sub(2, 0)
    take(3)
    nrm_own.wait()
    turn(dp)
    nrm_wait(x, 1 - c)
    turn(x * 2 + 1 - c)
    sub(1, 1)
    sub(2, 1)
    take(4)
    sub(3, 0)
    sub(4, 0)
    take(5)
    sub(3, 1)
    sub(4, 1)
    for way in range(2):
        wx_in(way, 0).wait_recv()
        wx_fw(way).start()
    for cc in range(2):
        nrm_wait(xp(1), cc)
        turn(xp(1) * 2 + cc)
    take(6)
    wc_in(0).wait_recv()
    add_states((dp, x * 2 + 1 - c))
    sub(5, 0)
    sub(6, 0)
    take(7)
    sub(5, 1)
    sub(6, 1)
    for cc in range(2):
        far_out(cc).start()
    for way in range(2):
        wx_in(way, 1).wait_recv()
    wc_out(1).start()
    wc_out(3).start()
    add_states((xp(1) * 2 + c, xp(-1) * 2 + c))
    for cc in range(2):
        nrm_wait(xp(3), cc)
        turn(xp(3) * 2 + cc)
    def power(j):
        rows = urows(j)
        row = sq_s[z, pl.ds(j, 1), :]
        for d in range(1, 8):
            row = row + sq_r[zp(d), pl.ds(j, 1), :]
        target = total[rows, :] * lax.rsqrt(to_col(row) / DT + norm_eps)
        total[rows, :] = target
        pow_s[j, 0:1, :] = to_row(jnp.sum(target * target, axis=1, keepdims=True))
        pow_cp(j).start()

    def pow_cp(j):
        return rc(pow_s.at[j], pow_r.at[j], pow_ss.at[j], pow_rs.at[j], grp_dev)

    sub(7, 0)
    for d in range(1, 8):
        sq_in(d).wait_recv()
    power(g)
    wx_fin(0).wait_recv()
    wx_fin(1).wait_recv()
    wc_out(2).start()
    sub(7, 1)
    power(1 - g)
    wc_in(1).wait_recv()
    wc_in(3).wait_recv()
    add_states((xp(1) * 2 + 1 - c, xp(-1) * 2 + 1 - c))
    far_in(c).wait_recv()
    swap_out(c).start()
    wc_in(2).wait_recv()
    add_states((xp(2) * 2, xp(2) * 2 + 1))

    def wal_out(q, e, u):
        b = wall.at[q, dp, urows(u), :]
        return rc(b, b, wal_ss.at[q, e - 1, u], wal_rs.at[q, e - 1, u], at(xx=xp(e)))

    def wal_in(q, e, u):
        b = wall.at[q, xp(-e) * 2 + c, urows(u), :]
        return rc(b, b, wal_ss.at[q, e - 1, u], wal_rs.at[q, e - 1, u], at(xx=xp(e)))

    def wac_out(q, e, u):
        b = wall.at[q, xp(-e) * 2 + c, urows(u), :]
        return rc(b, b, wac_ss.at[q, e, u], wac_rs.at[q, e, u], core_dev)

    def wac_wait(q, e):
        for u in range(2):
            b = wall.at[q, xp(-e) * 2 + 1 - c, urows(u), :]
            rc(b, b, wac_ss.at[q, e, u], wac_rs.at[q, e, u], core_dev).wait_recv()

    def pass_on(q, e):
        for j in (1 - g, g):
            wal_in(q, e, j).wait_recv()
            wac_out(q, e, j).start()

    def grad_out(q, t):
        to = lax.rem(mp + t, 16)
        return rc(
            grad_s.at[q, to], grad_r.at[q, mp], grad_ss.at[q, to], grad_rs.at[q, mp], (g, dp, to)
        )

    def grad_in(q, t):
        fr = lax.rem(mp + t, 16)
        return rc(
            grad_r.at[q, fr], grad_r.at[q, fr], grad_ss.at[q, fr], grad_rs.at[q, fr], (g, dp, fr)
        )

    def weigh(q, j, div):
        rows, cols = urows(j), slice(q * QW, q * QW + QW)
        wall[q, dp, rows, :] = ((states[rows, cols] - total[rows, cols]) / div).astype(BF16)
        for e in (1, 3, 2):
            wal_out(q, e, j).start()
        wac_out(q, 0, j).start()

    divs = []
    for j in (1 - g, g):
        pow_cp(j).wait_recv()
        power_j = (pow_s[j, 0:1, :] + pow_r[j, 0:1, :]) / KV + power_eps
        start = pl.multiple_of((mp % 4) * 256 + j * 128, 128)
        divs.append(to_col(len_row[0:1, pl.ds(start, 128)] * power_j))
        weigh(0, j, divs[-1])
    for q in range(1, NQ):
        for j, div in zip((1 - g, g), divs):
            weigh(q, j, div)
    far_in(1 - c).wait_recv()
    swap_out(1 - c).start()

    def accumulate(q, slot):
        grad[q % 2] += jnp.dot(nturn[slot], wall[q, slot], preferred_element_type=F32)

    def begin(q):
        grad[q % 2] = jnp.zeros((512, QW), F32)
        accumulate(q, dp)
        wac_wait(q, 0)
        accumulate(q, x * 2 + 1 - c)

    begin(0)
    for q in range(NQ):
        for e in (1, 3):
            pass_on(q, e)
        accumulate(q, xp(-1) * 2 + c)
        accumulate(q, xp(-3) * 2 + c)
        if q == 0:
            for cc in range(2):
                swap_in(cc).wait_recv()
                turn(xp(2) * 2 + cc)
        pass_on(q, 2)
        accumulate(q, xp(-2) * 2 + c)
        for e in (1, 3):
            wac_wait(q, e)
            accumulate(q, xp(-e) * 2 + 1 - c)
        if q + 1 < NQ:
            begin(q + 1)
        wac_wait(q, 2)
        accumulate(q, xp(-2) * 2 + 1 - c)
        for b in range(16):
            grad_s[q, b] = grad[q % 2, b * 32 : (b + 1) * 32, :].astype(BF16)
        for t in range(1, 16):
            grad_out(q, t).start()
        out_ref[:, q * QW : q * QW + QW] = grad[q % 2, pl.ds(pl.multiple_of(mp * 32, 32), 32), :]

    for q in range(NQ):
        for t in range(1, 16):
            grad_in(q, t).wait_recv()
        acc = out_ref[:, q * QW : q * QW + QW]
        for t in range(1, 16):
            acc = acc + grad_r[q, lax.rem(mp + t, 16)].astype(F32)
        out_ref[:, q * QW : q * QW + QW] = acc

    val_cp.wait_send()
    for e in range(4):
        if e > 0:
            vx_out(e).wait_send()
        vc_out(e).wait_send()
    gain_cp.wait_send()
    w_far.wait_send()
    for u in range(2):
        pow_cp(u).wait_send()
    for i in range(8):
        hid_out[i].wait_send()
        fwd_out[i].wait_send()
    for d in NEAR:
        wz_out(0, d).wait_send()
        wz_out(1, d).wait_send()
    for s in range(4):
        for u in range(2):
            ring_cp(0, s, u).wait_send()
            ring_cp(1, s, u).wait_send()
    for way in range(2):
        wx_out(way, 0).wait_send()
        wx_out(way, 1).wait_send()
        wx_fw(way).wait_send()
    for e in range(4):
        wc_out(e).wait_send()
        for q in range(NQ):
            for u in range(2):
                wac_out(q, e, u).wait_send()
    nrm_out(x, 1 - c, 0).wait_send()
    nrm_out(x, 1 - c, 1).wait_send()
    for cc in range(2):
        swap_out(cc).wait_send()
    for e in range(1, 4):
        for q in range(NQ):
            for u in range(2):
                wal_out(q, e, u).wait_send()
        for cc in range(2):
            if e == 2:
                far_out(cc).wait_send()
            else:
                nrm_out(xp(e), cc, 0).wait_send()
                nrm_out(xp(e), cc, 1).wait_send()
    for d in range(1, 8):
        sq_out(d).wait_send()
    for q in range(NQ):
        for t in range(1, 16):
            grad_out(q, t).wait_send()


def per_device(
    teacher_hidden,
    teacher_gain,
    teacher_value,
    student_hidden,
    student_gain,
    student_value,
    segment_ids,
):
    vmem = pl.BlockSpec(memory_space=pltpu.VMEM)
    dma = pltpu.SemaphoreType.DMA
    return pl.pallas_call(
        kernel,
        out_shape=pltpu.VMEM((32, 512), F32),
        in_specs=[pl.BlockSpec(memory_space=pl.ANY)] * 7,
        out_specs=vmem,
        scratch_shapes=[
            pltpu.VMEM((512,), BF16),
            pltpu.VMEM((512, 512), BF16),
            pltpu.VMEM((256, 4096), BF16),
            pltpu.VMEM((4096,), BF16),
            pltpu.VMEM((4, 1024), jnp.int32),
            pltpu.VMEM((2048, 512), BF16),
            pltpu.VMEM((2048, 512), BF16),
            pltpu.VMEM((512, 512), BF16),
            pltpu.VMEM((512,), BF16),
            pltpu.VMEM((8, 256, 512), BF16),
            pltpu.VMEM((8, 256, 512), BF16),
            pltpu.VMEM((8, 512, 256), BF16),
            pltpu.VMEM((8, 2, 256, 512), BF16),
            pltpu.VMEM((2, 4, 256, 512), BF16),
            pltpu.VMEM((2, 4, 256, 512), BF16),
            pltpu.VMEM((8, 8, 128), F32),
            pltpu.VMEM((8, 8, 128), F32),
            pltpu.VMEM((256, 512), F32),
            pltpu.VMEM((256, 512), F32),
            pltpu.VMEM((2, 8, 128), F32),
            pltpu.VMEM((2, 8, 128), F32),
            pltpu.VMEM((8, 1024), F32),
            pltpu.VMEM((NQ, 8, 256, QW), BF16),
            pltpu.VMEM((2, 512, QW), F32),
            pltpu.VMEM((NQ, 16, 32, QW), BF16),
            pltpu.VMEM((NQ, 16, 32, QW), BF16),
            dma((8,)),
            dma((8,)),
            dma((8,)),
            dma((8,)),
            dma((8,)),
            dma((5,)),
            dma((5,)),
            dma((4,)),
            dma((4,)),
            dma((4,)),
            dma((4,)),
            dma((2, 8)),
            dma((2, 8)),
            dma((3, 2)),
            dma((3, 2)),
            dma((4,)),
            dma((4,)),
            dma((8, 2)),
            dma((8, 2)),
            dma((2,)),
            dma((2,)),
            dma((2,)),
            dma((2,)),
            dma((2, 4, 2)),
            dma((2, 4, 2)),
            dma((8,)),
            dma((8,)),
            dma((NQ, 3, 2)),
            dma((NQ, 3, 2)),
            dma((NQ, 4, 2)),
            dma((NQ, 4, 2)),
            dma((NQ, 16)),
            dma((NQ, 16)),
        ],
        compiler_params=pltpu.CompilerParams(
            collective_id=0, has_side_effects=True, vmem_limit_bytes=56 * 1024 * 1024
        ),
    )(
        teacher_hidden,
        teacher_gain,
        teacher_value,
        student_hidden,
        student_gain,
        student_value,
        segment_ids,
    )


def solution(mesh):
    return jax.shard_map(
        per_device,
        mesh=mesh,
        in_specs=(
            P("dp", "mp"),
            P("mp"),
            P("mp", "grp"),
            P(("dp", "mp"), None),
            P(),
            P(("dp", "mp"), "grp"),
            P("dp", None),
        ),
        out_specs=P(("dp", "mp"), "grp"),
        check_vma=False,
    )
```

```python
import jax
import jax.numpy as jnp
from jax import lax
from jax.experimental import pallas as pl
from jax.experimental.pallas import tpu as pltpu
from jax.sharding import PartitionSpec as P

DT = 8192
DS = 4096
KV = 1024
NSEG = 8
MESH = pl.DeviceIdType.MESH
F32 = jnp.float32
BF16 = jnp.bfloat16

norm_eps = 1e-05
power_eps = 1e-06

ORDER = (4, 3, -3, 2, -2, 1, -1, 0)
NHID = 2
NQ = 4
QW = 512 // NQ
NEAR = (4, 3, -3, 2, -2, 1, -1)

PEERS = [(o, d) for d in NEAR + (0,) for o in (1, 0) if (o, d) != (0, 0)]


def kernel(
    hid_ref,
    gain_in,
    val_in,
    stu_in,
    sgain_in,
    wsh_ref,
    seg_in,
    out_ref,
    gain_ref,
    val_ref,
    stu_ref,
    sgain_ref,
    seg_ref,
    own,
    oth,
    valo,
    gaino,
    nrm,
    nall,
    nturn,
    wgt,
    ring_s,
    ring_r,
    sq_s,
    sq_r,
    states,
    total,
    pow_s,
    pow_r,
    len_row,
    wall,
    grad,
    grad_s,
    grad_r,
    loc_sem,
    hid_ss,
    hid_rs,
    fwd_ss,
    fwd_rs,
    misc_ss,
    misc_rs,
    vx_ss,
    vx_rs,
    vc_ss,
    vc_rs,
    wz_ss,
    wz_rs,
    wx_ss,
    wx_rs,
    wc_ss,
    wc_rs,
    nrm_ss,
    nrm_rs,
    swap_ss,
    swap_rs,
    pow_ss,
    pow_rs,
    ring_ss,
    ring_rs,
    sq_ss,
    sq_rs,
    wal_ss,
    wal_rs,
    wac_ss,
    wac_rs,
    grad_ss,
    grad_rs,
):
    g = lax.axis_index("grp")
    dp = lax.axis_index("dp")
    mp = lax.axis_index("mp")
    x, c = dp // 2, dp % 2
    h, z = mp // 8, mp % 8

    def at(grp=None, xx=None, cc=None, hh=None, zz=None):
        return (
            g if grp is None else grp,
            (x if xx is None else xx) * 2 + (c if cc is None else cc),
            (h if hh is None else hh) * 8 + (z if zz is None else zz),
        )

    def rc(src, dst, ss, rs, dev):
        return pltpu.make_async_remote_copy(
            src_ref=src, dst_ref=dst, send_sem=ss, recv_sem=rs, device_id=dev, device_id_type=MESH
        )

    zp = lambda d: lax.rem(z + d + 8, 8)
    xp = lambda e: lax.rem(x + e + 4, 4)
    grp_dev = at(grp=1 - g)
    cross_dev = at(grp=1 - g, hh=1 - h)
    far_dev = at(hh=1 - h)
    core_dev = at(cc=1 - c)

    own_cp = pltpu.make_async_copy(
        hid_ref.at[pl.ds(pl.multiple_of(h * 2048, 2048), 2048), :], own, loc_sem.at[0]
    )
    w_cp = pltpu.make_async_copy(
        wsh_ref, wgt.at[dp, h, pl.ds(pl.multiple_of(z * 32, 32), 32), :], loc_sem.at[1]
    )
    w_cp.start()
    gain_ld = pltpu.make_async_copy(gain_in, gain_ref, loc_sem.at[3])
    val_ld = pltpu.make_async_copy(val_in, val_ref, loc_sem.at[4])
    stu_ld = pltpu.make_async_copy(stu_in, stu_ref, loc_sem.at[5])
    sgain_ld = pltpu.make_async_copy(sgain_in, sgain_ref, loc_sem.at[6])
    seg_ld = pltpu.make_async_copy(seg_in, seg_ref, loc_sem.at[7])
    for ld in (stu_ld, sgain_ld, seg_ld, gain_ld, val_ld):
        ld.start()
    own_cp.start()

    barrier = pltpu.get_barrier_semaphore()
    count = 0
    for d in range(1, 8):
        pl.semaphore_signal(barrier, inc=1, device_id=at(zz=zp(d)), device_id_type=MESH)
        count += 1
    for d in range(8):
        pl.semaphore_signal(barrier, inc=1, device_id=at(hh=1 - h, zz=zp(d)), device_id_type=MESH)
        count += 1
    for e in range(1, 4):
        for cc in range(2):
            pl.semaphore_signal(
                barrier, inc=1, device_id=at(xx=xp(e), cc=cc), device_id_type=MESH
            )
            count += 1
    for dev in (grp_dev, cross_dev, core_dev):
        pl.semaphore_signal(barrier, inc=1, device_id=dev, device_id_type=MESH)
        count += 1

    pl.semaphore_wait(barrier, count)

    def wz_piece(hh, d):
        return wgt.at[dp, hh, pl.ds(pl.multiple_of(zp(d) * 32, 32), 32), :]

    def wz_out(b, d):
        src = wsh_ref if b == 0 else wz_piece(1 - h, 0)
        dst = wz_piece(h if b == 0 else 1 - h, 0)
        return rc(src, dst, wz_ss.at[b, zp(d)], wz_rs.at[b, z], at(zz=zp(d)))

    def wz_in(b, d):
        piece = wz_piece(h if b == 0 else 1 - h, d)
        return rc(piece, piece, wz_ss.at[b, zp(d)], wz_rs.at[b, zp(d)], at(zz=zp(d)))

    wrow = lambda hh: wz_piece(hh, 0)
    w_far = rc(wsh_ref, wrow(h), misc_ss.at[3], misc_rs.at[3], far_dev)
    w_far_in = rc(wsh_ref, wrow(1 - h), misc_ss.at[3], misc_rs.at[3], far_dev)
    w_far.start()
    def vblock(xx, cc):
        return valo.at[pl.ds(pl.multiple_of((xx * 2 + cc) * 64, 64), 64), :]

    val_cp = rc(
        val_in.at[pl.ds(pl.multiple_of(dp * 64, 64), 64), :],
        vblock(x, c),
        misc_ss.at[0],
        misc_rs.at[0],
        far_dev,
    )
    val_cp.start()

    def vx_out(e):
        b = vblock(x, c)
        return rc(b, b, vx_ss.at[e], vx_rs.at[e], at(xx=xp(e)))

    def vx_in(e):
        b = vblock(xp(-e), c)
        return rc(b, b, vx_ss.at[e], vx_rs.at[e], at(xx=xp(e)))

    def vc_out(e):
        b = vblock(xp(-e), c)
        return rc(b, b, vc_ss.at[e], vc_rs.at[e], core_dev)

    def vc_in(e):
        b = vblock(xp(-e), 1 - c)
        return rc(b, b, vc_ss.at[e], vc_rs.at[e], core_dev)

    gain_cp = rc(gain_in, gaino, misc_ss.at[2], misc_rs.at[2], cross_dev)
    gain_cp.start()

    def hid_rows(hh, i, j):
        return pl.ds(pl.multiple_of(hh * 2048 + zp(ORDER[i]) * 256 + j * 128, 128), 128)

    def loc_rows(i, j):
        return pl.ds(pl.multiple_of(zp(ORDER[i]) * 256 + j * 128, 128), 128)

    hid_out, hid_in, fwd_out, fwd_in = [], [], [], []
    for i in range(8):
        hid_out.append(
            rc(
                hid_ref.at[hid_rows(1 - h, i, 1 - g), :],
                oth.at[loc_rows(i, 1 - g), :],
                hid_ss.at[i],
                hid_rs.at[i],
                cross_dev,
            )
        )
        mine = oth.at[loc_rows(i, g), :]
        theirs = oth.at[loc_rows(i, 1 - g), :]
        hid_in.append(rc(mine, mine, hid_ss.at[i], hid_rs.at[i], cross_dev))
        fwd_out.append(rc(mine, mine, fwd_ss.at[i], fwd_rs.at[i], grp_dev))
        fwd_in.append(rc(theirs, theirs, fwd_ss.at[i], fwd_rs.at[i], grp_dev))
    for d in NEAR:
        wz_out(0, d).start()
    for i in range(NHID):
        hid_out[i].start()

    def nrm_out(xx, cc, part):
        to, rows = xx * 2 + cc, pl.ds(part * 128, 128)
        return rc(
            nrm.at[to, rows, :],
            nall.at[dp, rows, :],
            nrm_ss.at[to, part],
            nrm_rs.at[dp, part],
            at(xx=xx, cc=cc),
        )

    def nrm_wait(xx, cc):
        fr = xx * 2 + cc
        for part in range(2):
            b = nall.at[fr, pl.ds(part * 128, 128), :]
            rc(b, b, nrm_ss.at[fr, part], nrm_rs.at[fr, part], at(xx=xx, cc=cc)).wait_recv()

    grows = lambda gg: pl.ds(pl.multiple_of(gg * 128, 128), 128)

    def far_out(cc):
        to = xp(2) * 2 + cc
        return rc(
            nrm.at[to, grows(g), :],
            nall.at[dp, grows(g), :],
            nrm_ss.at[to, 0],
            nrm_rs.at[dp, 0],
            at(xx=xp(2), cc=cc),
        )

    def far_in(cc):
        b = nall.at[xp(2) * 2 + cc, grows(g), :]
        return rc(b, b, nrm_ss.at[xp(2) * 2 + cc, 0], nrm_rs.at[xp(2) * 2 + cc, 0], grp_dev)

    def swap_out(cc):
        b = nall.at[xp(2) * 2 + cc, grows(g), :]
        return rc(b, b, swap_ss.at[cc], swap_rs.at[cc], grp_dev)

    def swap_in(cc):
        b = nall.at[xp(2) * 2 + cc, grows(1 - g), :]
        return rc(b, b, swap_ss.at[cc], swap_rs.at[cc], grp_dev)

    stu_ld.wait()
    sgain_ld.wait()
    sgain = sgain_ref[...].astype(F32).reshape(1, DS)

    @pl.loop(0, 8)
    def _(i):
        rows = pl.ds(pl.multiple_of(i * 32, 32), 32)
        wide = stu_ref[rows, :].astype(F32)
        scale = lax.rsqrt(jnp.sum(wide * wide, axis=1, keepdims=True) / DS + norm_eps)
        done = (wide * scale * sgain).astype(BF16)
        for b in range(8):
            nrm[b, rows, :] = done[:, b * 512 : (b + 1) * 512]

    nrm_own = pltpu.make_async_copy(nrm.at[dp], nall.at[dp], loc_sem.at[2])
    nrm_own.start()

    seg_ld.wait()
    seg = seg_ref[pl.ds(mp // 4, 1), :]
    lens = jnp.zeros((1, 1024), F32)
    for s in range(NSEG):
        hit = (seg == s).astype(F32)
        lens = lens + hit * jnp.sum(hit, axis=1, keepdims=True)
    len_row[0:1, :] = lens

    eye = lax.broadcasted_iota(jnp.int32, (128, 128), 0) == lax.broadcasted_iota(
        jnp.int32, (128, 128), 1
    )

    def to_row(col):
        return jnp.sum(jnp.where(eye, col, 0.0), axis=0, keepdims=True)

    def to_col(row):
        return jnp.sum(jnp.where(eye, row, 0.0), axis=1, keepdims=True)

    for e in (1, 3):
        nrm_out(xp(e), c, 0).start()
    for part in range(2):
        nrm_out(x, 1 - c, part).start()

    def wblock(xx, cc=None):
        return wgt.at[xx * 2 + (c if cc is None else cc)]

    def wx_dev(way):
        return at(xx=xp(1 if way == 0 else -1))

    def wx_out(way, part):
        b = wblock(x).at[way if part == 0 else 1 - way]
        return rc(b, b, wx_ss.at[part, way], wx_rs.at[part, way], wx_dev(way))

    def wx_in(way, part):
        b = wblock(xp(-1 if way == 0 else 1)).at[way if part == 0 else 1 - way]
        return rc(b, b, wx_ss.at[part, way], wx_rs.at[part, way], wx_dev(way))

    def wx_fw(way):
        b = wblock(xp(-1 if way == 0 else 1)).at[way]
        return rc(b, b, wx_ss.at[2, way], wx_rs.at[2, way], wx_dev(way))

    def wx_fin(way):
        b = wblock(xp(2)).at[way]
        return rc(b, b, wx_ss.at[2, way], wx_rs.at[2, way], wx_dev(way))

    def wc_out(e):
        b = wblock(xp(e))
        return rc(b, b, wc_ss.at[e], wc_rs.at[e], core_dev)

    def wc_in(e):
        b = wblock(xp(e), 1 - c)
        return rc(b, b, wc_ss.at[e], wc_rs.at[e], core_dev)

    jrow = lambda u: g if u == 0 else 1 - g
    urows = lambda j: pl.ds(pl.multiple_of(j * 128, 128), 128)

    def ring_cp(way, s, u):
        rows = urows(jrow(u))
        cols = pl.ds(way * 256, 256) if s == 0 else pl.ds(0, 512)
        dev = at(zz=zp(1 if way == 0 else -1))
        return rc(
            ring_s.at[way, s, rows, cols],
            ring_r.at[way, s, rows, cols],
            ring_ss.at[way, s, u],
            ring_rs.at[way, s, u],
            dev,
        )

    def sq_out(d):
        return rc(sq_s.at[zp(d)], sq_r.at[z], sq_ss.at[zp(d)], sq_rs.at[z], at(zz=zp(d)))

    def sq_in(d):
        return rc(sq_r.at[zp(d)], sq_r.at[zp(d)], sq_ss.at[zp(d)], sq_rs.at[zp(d)], at(zz=zp(d)))

    def sub(i, u):
        d = ORDER[i]
        k = zp(d)
        j = jrow(u)
        if u == 1:
            fwd_in[i].wait_recv()
        if d == 0:
            ring_cp(0, 3, u).wait_recv()
            ring_cp(1, 3, u).wait_recv()
        elif d != 4:
            ring_cp(0 if d > 0 else 1, 3 - abs(d), u).wait_recv()
        rows = pl.ds(pl.multiple_of(k * 256 + j * 128, 128), 128)
        brows = urows(j)
        h1 = own[rows, :].astype(F32)
        h2 = oth[rows, :].astype(F32)
        tgain = gain_ref[...].astype(F32).reshape(1, 512)
        tgaino = gaino[...].astype(F32).reshape(1, 512)
        acc = jnp.dot((h1 * tgain).astype(BF16), val_ref[...], preferred_element_type=F32)
        acc += jnp.dot((h2 * tgaino).astype(BF16), valo[...], preferred_element_type=F32)
        sq = jnp.sum(h1 * h1 + h2 * h2, axis=1, keepdims=True)
        sq_s[k, pl.ds(j, 1), :] = to_row(sq)
        if u == 1 and d != 0:
            sq_out(d).start()
        if d == 4:
            ring_s[0, 0, brows, 0:256] = acc[:, 0:256].astype(BF16)
            ring_s[1, 0, brows, 256:512] = acc[:, 256:512].astype(BF16)
            ring_cp(0, 0, u).start()
            ring_cp(1, 0, u).start()
        elif d == 0:
            total[brows, :] = (
                acc + ring_r[0, 3, brows, :].astype(F32) + ring_r[1, 3, brows, :].astype(F32)
            )
        else:
            way, s = (0 if d > 0 else 1), 4 - abs(d)
            if s == 1:
                cols = slice(way * 256, way * 256 + 256)
                rest = slice((1 - way) * 256, (1 - way) * 256 + 256)
                ring_s[way, s, brows, cols] = (
                    acc[:, cols] + ring_r[way, 0, brows, cols].astype(F32)
                ).astype(BF16)
                ring_s[way, s, brows, rest] = acc[:, rest].astype(BF16)
            else:
                ring_s[way, s, brows, :] = (
                    acc + ring_r[way, s - 1, brows, :].astype(F32)
                ).astype(BF16)
            ring_cp(way, s, u).start()

    def turn(slot):
        nturn[slot] = nall[slot].T

    def take(i):
        hid_in[i].wait_recv()
        fwd_out[i].start()

    def add_states(blocks):
        part = None
        for b in blocks:
            for hh in range(2):
                t = jnp.dot(
                    nrm[b, :, hh * 256 : hh * 256 + 256], wgt[b, hh], preferred_element_type=F32
                )
                part = t if part is None else part + t
        states[...] += part

    states[...] = jnp.zeros_like(states)
    val_cp.wait_recv()
    for e in (2, 1, 3):
        vx_out(e).start()
    vc_out(0).start()
    for e in (1, 3):
        nrm_out(xp(e), c, 1).start()
    for part in range(2):
        for e in (1, 3):
            nrm_out(xp(e), 1 - c, part).start()
    for i in range(NHID, 8):
        hid_out[i].start()
    w_far_in.wait_recv()
    for d in NEAR:
        wz_out(1, d).start()
    take(0)
    for e in (1, 3, 2):
        vx_in(e).wait_recv()
        vc_out(e).start()
    own_cp.wait()
    w_cp.wait()
    gain_ld.wait()
    val_ld.wait()
    gain_cp.wait_recv()
    take(1)
    for e in range(4):
        vc_in(e).wait_recv()
    sub(0, 0)
    sub(0, 1)
    for b in range(2):
        for d in NEAR:
            wz_in(b, d).wait_recv()
    for part in range(2):
        for way in range(2):
            wx_out(way, part).start()
    wc_out(0).start()
    take(2)
    sub(1, 0)
    sub(2, 0)
    take(3)
    nrm_own.wait()
    turn(dp)
    nrm_wait(x, 1 - c)
    turn(x * 2 + 1 - c)
    sub(1, 1)
    sub(2, 1)
    take(4)
    sub(3, 0)
    sub(4, 0)
    take(5)
    sub(3, 1)
    sub(4, 1)
    for way in range(2):
        wx_in(way, 0).wait_recv()
        wx_fw(way).start()
    for cc in range(2):
        nrm_wait(xp(1), cc)
        turn(xp(1) * 2 + cc)
    take(6)
    wc_in(0).wait_recv()
    add_states((dp, x * 2 + 1 - c))
    sub(5, 0)
    sub(6, 0)
    take(7)
    sub(5, 1)
    sub(6, 1)
    for cc in range(2):
        far_out(cc).start()
    for way in range(2):
        wx_in(way, 1).wait_recv()
    wc_out(1).start()
    wc_out(3).start()
    add_states((xp(1) * 2 + c, xp(-1) * 2 + c))
    for cc in range(2):
        nrm_wait(xp(3), cc)
        turn(xp(3) * 2 + cc)
    def power(j):
        rows = urows(j)
        row = sq_s[z, pl.ds(j, 1), :]
        for d in range(1, 8):
            row = row + sq_r[zp(d), pl.ds(j, 1), :]
        target = total[rows, :] * lax.rsqrt(to_col(row) / DT + norm_eps)
        total[rows, :] = target
        pow_s[j, 0:1, :] = to_row(jnp.sum(target * target, axis=1, keepdims=True))
        pow_cp(j).start()

    def pow_cp(j):
        return rc(pow_s.at[j], pow_r.at[j], pow_ss.at[j], pow_rs.at[j], grp_dev)

    sub(7, 0)
    for d in range(1, 8):
        sq_in(d).wait_recv()
    power(g)
    wx_fin(0).wait_recv()
    wx_fin(1).wait_recv()
    wc_out(2).start()
    sub(7, 1)
    power(1 - g)
    wc_in(1).wait_recv()
    wc_in(3).wait_recv()
    add_states((xp(1) * 2 + 1 - c, xp(-1) * 2 + 1 - c))
    far_in(c).wait_recv()
    swap_out(c).start()
    wc_in(2).wait_recv()
    add_states((xp(2) * 2, xp(2) * 2 + 1))

    def wal_out(q, e, u):
        b = wall.at[q, dp, urows(u), :]
        return rc(b, b, wal_ss.at[q, e - 1, u], wal_rs.at[q, e - 1, u], at(xx=xp(e)))

    def wal_in(q, e, u):
        b = wall.at[q, xp(-e) * 2 + c, urows(u), :]
        return rc(b, b, wal_ss.at[q, e - 1, u], wal_rs.at[q, e - 1, u], at(xx=xp(e)))

    def wac_out(q, e, u):
        b = wall.at[q, xp(-e) * 2 + c, urows(u), :]
        return rc(b, b, wac_ss.at[q, e, u], wac_rs.at[q, e, u], core_dev)

    def wac_wait(q, e):
        for u in range(2):
            b = wall.at[q, xp(-e) * 2 + 1 - c, urows(u), :]
            rc(b, b, wac_ss.at[q, e, u], wac_rs.at[q, e, u], core_dev).wait_recv()

    def pass_on(q, e):
        for j in (1 - g, g):
            wal_in(q, e, j).wait_recv()
            wac_out(q, e, j).start()

    def peer(t):
        other, d = PEERS[t]
        return (1 - h if other else h) * 8 + zp(d)

    def grad_out(q, t):
        to = peer(t)
        return rc(
            grad_s.at[q, to], grad_r.at[q, mp], grad_ss.at[q, to], grad_rs.at[q, mp], (g, dp, to)
        )

    def grad_in(q, t):
        fr = peer(t)
        return rc(
            grad_r.at[q, fr], grad_r.at[q, fr], grad_ss.at[q, fr], grad_rs.at[q, fr], (g, dp, fr)
        )

    def weigh(q, j, div):
        rows, cols = urows(j), slice(q * QW, q * QW + QW)
        wall[q, dp, rows, :] = ((states[rows, cols] - total[rows, cols]) / div).astype(BF16)
        for e in (1, 3, 2):
            wal_out(q, e, j).start()
        wac_out(q, 0, j).start()

    divs = []
    for j in (1 - g, g):
        pow_cp(j).wait_recv()
        power_j = (pow_s[j, 0:1, :] + pow_r[j, 0:1, :]) / KV + power_eps
        start = pl.multiple_of((mp % 4) * 256 + j * 128, 128)
        divs.append(to_col(len_row[0:1, pl.ds(start, 128)] * power_j))
        weigh(0, j, divs[-1])
    for q in range(1, NQ):
        for j, div in zip((1 - g, g), divs):
            weigh(q, j, div)
    far_in(1 - c).wait_recv()
    swap_out(1 - c).start()

    def accumulate(q, slot):
        grad[q % 2] += jnp.dot(nturn[slot], wall[q, slot], preferred_element_type=F32)

    def begin(q):
        grad[q % 2] = jnp.zeros((512, QW), F32)
        accumulate(q, dp)
        wac_wait(q, 0)
        accumulate(q, x * 2 + 1 - c)

    begin(0)
    for q in range(NQ):
        for e in (1, 3):
            pass_on(q, e)
        accumulate(q, xp(-1) * 2 + c)
        accumulate(q, xp(-3) * 2 + c)
        if q == 0:
            for cc in range(2):
                swap_in(cc).wait_recv()
                turn(xp(2) * 2 + cc)
        pass_on(q, 2)
        accumulate(q, xp(-2) * 2 + c)
        for e in (1, 3):
            wac_wait(q, e)
            accumulate(q, xp(-e) * 2 + 1 - c)
        if q + 1 < NQ:
            begin(q + 1)
        wac_wait(q, 2)
        accumulate(q, xp(-2) * 2 + 1 - c)
        for b in range(16):
            grad_s[q, b] = grad[q % 2, b * 32 : (b + 1) * 32, :].astype(BF16)
        for t in range(15):
            grad_out(q, t).start()
        out_ref[:, q * QW : q * QW + QW] = grad[q % 2, pl.ds(pl.multiple_of(mp * 32, 32), 32), :]

    for q in range(NQ):
        for t in range(15):
            grad_in(q, t).wait_recv()
        acc = out_ref[:, q * QW : q * QW + QW]
        for t in range(15):
            acc = acc + grad_r[q, peer(t)].astype(F32)
        out_ref[:, q * QW : q * QW + QW] = acc

    val_cp.wait_send()
    for e in range(4):
        if e > 0:
            vx_out(e).wait_send()
        vc_out(e).wait_send()
    gain_cp.wait_send()
    w_far.wait_send()
    for u in range(2):
        pow_cp(u).wait_send()
    for i in range(8):
        hid_out[i].wait_send()
        fwd_out[i].wait_send()
    for d in NEAR:
        wz_out(0, d).wait_send()
        wz_out(1, d).wait_send()
    for s in range(4):
        for u in range(2):
            ring_cp(0, s, u).wait_send()
            ring_cp(1, s, u).wait_send()
    for way in range(2):
        wx_out(way, 0).wait_send()
        wx_out(way, 1).wait_send()
        wx_fw(way).wait_send()
    for e in range(4):
        wc_out(e).wait_send()
        for q in range(NQ):
            for u in range(2):
                wac_out(q, e, u).wait_send()
    nrm_out(x, 1 - c, 0).wait_send()
    nrm_out(x, 1 - c, 1).wait_send()
    for cc in range(2):
        swap_out(cc).wait_send()
    for e in range(1, 4):
        for q in range(NQ):
            for u in range(2):
                wal_out(q, e, u).wait_send()
        for cc in range(2):
            if e == 2:
                far_out(cc).wait_send()
            else:
                nrm_out(xp(e), cc, 0).wait_send()
                nrm_out(xp(e), cc, 1).wait_send()
    for d in range(1, 8):
        sq_out(d).wait_send()
    for q in range(NQ):
        for t in range(15):
            grad_out(q, t).wait_send()


def per_device(
    teacher_hidden,
    teacher_gain,
    teacher_value,
    student_hidden,
    student_gain,
    student_value,
    segment_ids,
):
    vmem = pl.BlockSpec(memory_space=pltpu.VMEM)
    dma = pltpu.SemaphoreType.DMA
    return pl.pallas_call(
        kernel,
        out_shape=pltpu.VMEM((32, 512), F32),
        in_specs=[pl.BlockSpec(memory_space=pl.ANY)] * 7,
        out_specs=vmem,
        scratch_shapes=[
            pltpu.VMEM((512,), BF16),
            pltpu.VMEM((512, 512), BF16),
            pltpu.VMEM((256, 4096), BF16),
            pltpu.VMEM((4096,), BF16),
            pltpu.VMEM((4, 1024), jnp.int32),
            pltpu.VMEM((2048, 512), BF16),
            pltpu.VMEM((2048, 512), BF16),
            pltpu.VMEM((512, 512), BF16),
            pltpu.VMEM((512,), BF16),
            pltpu.VMEM((8, 256, 512), BF16),
            pltpu.VMEM((8, 256, 512), BF16),
            pltpu.VMEM((8, 512, 256), BF16),
            pltpu.VMEM((8, 2, 256, 512), BF16),
            pltpu.VMEM((2, 4, 256, 512), BF16),
            pltpu.VMEM((2, 4, 256, 512), BF16),
            pltpu.VMEM((8, 8, 128), F32),
            pltpu.VMEM((8, 8, 128), F32),
            pltpu.VMEM((256, 512), F32),
            pltpu.VMEM((256, 512), F32),
            pltpu.VMEM((2, 8, 128), F32),
            pltpu.VMEM((2, 8, 128), F32),
            pltpu.VMEM((8, 1024), F32),
            pltpu.VMEM((NQ, 8, 256, QW), BF16),
            pltpu.VMEM((2, 512, QW), F32),
            pltpu.VMEM((NQ, 16, 32, QW), BF16),
            pltpu.VMEM((NQ, 16, 32, QW), BF16),
            dma((8,)),
            dma((8,)),
            dma((8,)),
            dma((8,)),
            dma((8,)),
            dma((5,)),
            dma((5,)),
            dma((4,)),
            dma((4,)),
            dma((4,)),
            dma((4,)),
            dma((2, 8)),
            dma((2, 8)),
            dma((3, 2)),
            dma((3, 2)),
            dma((4,)),
            dma((4,)),
            dma((8, 2)),
            dma((8, 2)),
            dma((2,)),
            dma((2,)),
            dma((2,)),
            dma((2,)),
            dma((2, 4, 2)),
            dma((2, 4, 2)),
            dma((8,)),
            dma((8,)),
            dma((NQ, 3, 2)),
            dma((NQ, 3, 2)),
            dma((NQ, 4, 2)),
            dma((NQ, 4, 2)),
            dma((NQ, 16)),
            dma((NQ, 16)),
        ],
        compiler_params=pltpu.CompilerParams(
            collective_id=0, has_side_effects=True, vmem_limit_bytes=56 * 1024 * 1024
        ),
    )(
        teacher_hidden,
        teacher_gain,
        teacher_value,
        student_hidden,
        student_gain,
        student_value,
        segment_ids,
    )


def solution(mesh):
    return jax.shard_map(
        per_device,
        mesh=mesh,
        in_specs=(
            P("dp", "mp"),
            P("mp"),
            P("mp", "grp"),
            P(("dp", "mp"), None),
            P(),
            P(("dp", "mp"), "grp"),
            P("dp", None),
        ),
        out_specs=P(("dp", "mp"), "grp"),
        check_vma=False,
    )
```
